32 devices in a mesh: gx: 4 (over z), gy: 4 (over y, x), ma: 2 (over core).
Axes of the slice: x: 2, y: 2, z: 4, core: 2. Of those that a mesh axis runs over, the one named last changes fastest.
Arguments:
- perturbations: float32 [30, 2, 128, 2048], P('ma', None, 'gx', 'gy'), may hold values from -6 to 6
- coefficients: float32 [2, 128, 2048], P(None, 'gx', 'gy'), may hold values from 0.02 to 0.12
- coarse_coefficients: float32 [2, 32, 512], P(None, 'gx', 'gy'), may hold values from 0.02 to 0.12
- iterate: float32 [2, 128, 2048], P(None, 'gx', 'gy'), may hold values from -6 to 6
- residual: float32 [2, 128, 2048], P(None, 'gx', 'gy'), may hold values from -6 to 6
- direction: float32 [2, 128, 2048], P(None, 'gx', 'gy'), may hold values from -6 to 6
Outputs:
- new_iterate: float32 [2, 128, 2048], P(None, 'gx', 'gy')
- new_residual: float32 [2, 128, 2048], P(None, 'gx', 'gy')
- new_direction: float32 [2, 128, 2048], P(None, 'gx', 'gy')
The draws below stay inside these ranges and needn't reach their ends.
All inputs are finite; a program needn't handle non-finite values.
Results may differ from the reference program's by a relative error of at most 0.0001.
Values sent between devices are 32-bit elements; how exact they have to be, the bound alone decides.
A program may use at most 192 MiB of HBM per device.

```python
import jax
import jax.numpy as jnp
from jax import lax

MEMBERS = 30
LEV = 2
PASSES = 3
RATIO = 4
NX = 128
NY = 2048


def block_levels(rng, extent, shards, smallest, top_value):
    def one(axis_at, shards_of):
        steps = jax.random.uniform(jax.random.fold_in(jax.random.fold_in(rng, 6), axis_at), (shards_of,), jnp.float32, smallest / len(shards), top_value / len(shards))
        return jnp.repeat(jnp.exp(steps), extent[axis_at] // shards_of).reshape((-1,) + (1,) * (len(extent) - axis_at - 1))

    level = one(*shards[0])
    for cut in shards[1:]:
        level = level * one(*cut)
    return level


def scatter_about(stream_key, extent, spread, reach, shards=(), kind=jnp.bfloat16):
    values = jax.random.normal(stream_key, extent, jnp.float32) * spread
    if len(shards) > 0:
        values = block_levels(stream_key, extent, shards, -0.22, 0.18) * values
    return jnp.clip(values, min=-reach, max=reach).astype(kind)


def setup_inputs(seed: int = 0) -> dict:
    key_of = jax.random.split(jax.random.key(seed), 7)
    perturbations = scatter_about(key_of[0], (MEMBERS, LEV, NX, NY), 1.0, 6.0, ((0, 2), (2, 4), (3, 4)), jnp.float32)
    coefficients = jnp.clip(0.02 + 0.09999999776482582 * jax.random.uniform(key_of[1], (2, NX, NY), jnp.float32) ** block_levels(key_of[1], (2, NX, NY), ((1, 4), (2, 4)), -0.2, 0.2), 0.02, 0.12)
    coarse_coefficients = jnp.clip(0.02 + 0.09999999776482582 * jax.random.uniform(key_of[2], (2, NX // RATIO, NY // RATIO), jnp.float32) ** block_levels(key_of[2], (2, NX // RATIO, NY // RATIO), ((1, 4), (2, 4)), -0.2, 0.2), 0.02, 0.12)
    iterate = scatter_about(key_of[3], (LEV, NX, NY), 1.0, 6.0, ((1, 4), (2, 4)), jnp.float32)
    residual = scatter_about(key_of[4], (LEV, NX, NY), 1.0, 6.0, ((1, 4), (2, 4)), jnp.float32)
    direction = scatter_about(key_of[5], (LEV, NX, NY), 1.0, 6.0, ((1, 4), (2, 4)), jnp.float32)
    return {"perturbations": perturbations, "coefficients": coefficients, "coarse_coefficients": coarse_coefficients, "iterate": iterate, "residual": residual, "direction": direction}


def stencil_pass(source, coef_x, coef_y):
    centre = source[..., 1:-1, 1:-1]
    edge_x = 0.5 * (coef_x[1:, 1:-1] + coef_x[:-1, 1:-1])
    edge_y = 0.5 * (coef_y[1:-1, 1:] + coef_y[1:-1, :-1])
    along_x = edge_x[1:] * (source[..., 2:, 1:-1] - centre) - edge_x[:-1] * (centre - source[..., :-2, 1:-1])
    along_y = edge_y[:, 1:] * (source[..., 1:-1, 2:] - centre) - edge_y[:, :-1] * (centre - source[..., 1:-1, :-2])
    return centre + along_x + along_y


def smooth_level(source, coefficient_pair):
    padding = [(0, 0)] * (source.ndim - 2) + [(1, 1), (1, 1)]
    padded_coefs = jnp.pad(coefficient_pair, ((0, 0), (1, 1), (1, 1)))
    result = source
    for sweep_index in range(PASSES):
        result = stencil_pass(jnp.pad(result, padding), padded_coefs[0], padded_coefs[1])
    return result


def restrict_blocks(source):
    shaped = source.reshape(source.shape[:-2] + (source.shape[-2] // RATIO, RATIO, source.shape[-1] // RATIO, RATIO))
    return jnp.mean(shaped, axis=(-3, -1))


def prolong_blocks(source):
    return jnp.repeat(jnp.repeat(source, RATIO, axis=-2), RATIO, axis=-1)


def reference(perturbations, coefficients, coarse_coefficients, iterate, residual, direction):
    def add_member(running_sum, member):
        weighted = member * direction
        fine_part = smooth_level(weighted, coefficients)
        coarse_part = smooth_level(restrict_blocks(weighted), coarse_coefficients)
        localized = fine_part + prolong_blocks(coarse_part)
        return running_sum + member * localized, None

    running_sum, unused = lax.scan(add_member, jnp.zeros_like(direction), perturbations)
    operator_image = direction + running_sum / (MEMBERS - 1)
    norm_old = jnp.sum(residual * residual)
    step_length = norm_old / jnp.sum(direction * operator_image)
    new_iterate = iterate + step_length * direction
    new_residual = residual - step_length * operator_image
    norm_new = jnp.sum(new_residual * new_residual)
    new_direction = new_residual + (norm_new / norm_old) * direction
    return (new_iterate, new_residual, new_direction)
```

```python
import functools

import jax
import jax.numpy as jnp
from jax import lax
from jax.experimental import pallas as pl
from jax.experimental.pallas import tpu as pltpu
from jax.sharding import PartitionSpec as P

MEMBERS = 30
PASSES = 3
RATIO = 4
HALO = 4
LANES = 128
EDGE = 8
REACH = 3
PAIRS = (
    (0, 0), (0, 1), (0, 2), (0, 3), (1, 0), (2, 0), (3, 0), (1, 1), (1, 2), (2, 1),
    (-1, 1), (-1, 2), (-2, 1),
)
ACROSS = tuple((i, k) for i in (1, 2, 3) for k in range(i - 3, 4 - i))
ROWS = (-2, -1, 1, 2, 3)
MATRICES = tuple((0, True, k) for k in (1, 2)) + tuple((0, False, k) for k in (1, 2, 3))
MATRICES += tuple((1, True, k) for k in (1, 2, 3)) + tuple((1, False, k) for k in (1, 2))
COPIES = len(MATRICES)
MESH = pl.DeviceIdType.MESH
F32 = jnp.float32
BF16 = jnp.bfloat16


def shift_up(u, axis):
    return pltpu.roll(u, u.shape[axis] - 1, axis)


def shift_down(u, axis):
    return pltpu.roll(u, 1, axis)


def split_dot(a, b):
    high = a.astype(BF16)
    low = (a - high.astype(F32)).astype(BF16)
    return jnp.dot(high, b, preferred_element_type=F32) + jnp.dot(
        low, b, preferred_element_type=F32
    )


def stencil_weights(cx, cy, rows, cols, has_prev, has_next, has_left, has_right):
    ext_rows, ext_cols = cx.shape
    row = lax.broadcasted_iota(jnp.int32, (ext_rows, ext_cols), 0)
    col = lax.broadcasted_iota(jnp.int32, (ext_rows, ext_cols), 1)
    outside = (
        ((row >= rows) & (row < rows + HALO) & (has_next == 0))
        | ((row >= rows + HALO) & (has_prev == 0))
        | ((col >= cols) & (col < cols + LANES // 2) & (has_right == 0))
        | ((col >= cols + LANES // 2) & (has_left == 0))
    )
    xp = 0.5 * (cx + shift_up(cx, 0))
    xm = shift_down(xp, 0)
    yp = 0.5 * (cy + shift_up(cy, 1))
    ym = shift_down(yp, 1)
    centre = 1.0 - xp - xm - yp - ym
    return [jnp.where(outside, 0.0, value) for value in (centre, xp, xm, yp, ym)]


def apply_passes(u, weights):
    for _ in range(PASSES):
        u = (
            weights[0][...] * u
            + weights[1][...] * shift_up(u, 0)
            + weights[2][...] * shift_down(u, 0)
            + weights[3][...] * shift_up(u, 1)
            + weights[4][...] * shift_down(u, 1)
        )
    return u


def shifted(u, dx, dy):
    if dx:
        u = pltpu.roll(u, -dx % u.shape[0], 0)
    if dy:
        u = pltpu.roll(u, -dy % u.shape[1], 1)
    return u


def composite(cx, cy, inside):
    s = shifted
    half_x = 0.5 * (cx + s(cx, 1, 0))
    half_y = 0.5 * (cy + s(cy, 0, 1))
    d = inside * (1.0 - half_x - s(half_x, -1, 0) - half_y - s(half_y, 0, -1))
    x = inside * s(inside, 1, 0) * half_x
    y = inside * s(inside, 0, 1) * half_y
    x2, y2 = x * x, y * y
    q = x2 + s(x2, -1, 0) + y2 + s(y2, 0, -1)
    dx, dy, dm = s(d, 1, 0), s(d, 0, 1), s(d, 0, -1)
    dxx, dyy, dxy, dxm = s(d, 2, 0), s(d, 0, 2), s(dy, 1, 0), s(dm, 1, 0)
    xx1, xy1, xm1 = s(x, 1, 0), s(x, 0, 1), s(x, 0, -1)
    yx1, yy1, ym = s(y, 1, 0), s(y, 0, 1), s(y, 0, -1)
    ymx = s(ym, 1, 0)
    xx, yy, xy, yx = x * xx1, y * yy1, x * yx1, y * xy1
    xym, ymx_then, ymym = x * ymx, ym * xm1, s(yy, 0, -2)
    u = {}
    u[0, 0] = d * (d * d + 2.0 * q) + x2 * dx + s(x2 * d, -1, 0) + y2 * dy + s(y2 * d, 0, -1)
    u[1, 0] = x * (d * d + d * dx + dx * dx + q + s(q, 1, 0) - x2) + yx * yx1 + ymx_then * ymx
    u[0, 1] = y * (d * d + d * dy + dy * dy + q + s(q, 0, 1) - y2) + xy * xy1 + s(x * yx, -1, 0)
    u[2, 0] = xx * (d + dx + dxx)
    u[0, 2] = yy * (d + dy + dyy)
    u[3, 0] = xx * s(x, 2, 0)
    u[0, 3] = yy * s(y, 0, 2)
    u[1, 1] = xy * (d + dx + dxy) + yx * (d + dy + dxy)
    u[1, -1] = xym * (d + dx + dxm) + ymx_then * (d + dm + dxm)
    u[2, 1] = xx * s(y, 2, 0) + x * s(yx, 1, 0) + y * s(xx, 0, 1)
    u[2, -1] = xx * s(ymx, 1, 0) + x * s(ymx_then, 1, 0) + ym * s(xx, 0, -1)
    u[1, 2] = x * s(yy, 1, 0) + y * s(xy, 0, 1) + yy * s(x, 0, 2)
    u[1, -2] = x * s(ymym, 1, 0) + ym * s(xym, 0, -1) + ymym * s(x, 0, -2)
    return u


def kernel(
    sizes,
    p_hbm, coef_hbm, ccoef_hbm, r_hbm, d_hbm,
    q_ref, step_ref, growth_ref,
    pv, coef_ref, ccoef_ref, r_ref, d_ref,
    wc, line, lanes_out,
    c_top, c_bottom, strips,
    rx_next, rx_prev, rc_next, rc_prev, ry, rd,
    cb, hv, hyc, sums_ref, inner, weights, coarse_weights, dv, dk, ev, fv, mv, copies, totals,
    acc, acc_other, part, slots,
    load_sem, send_sem, recv_sem, group_send, group_recv,
):
    n_x, n_y = sizes
    levels, rows, cols = d_ref.shape
    half, tiles = pv.shape[0], cols // LANES
    crows, ccols = ccoef_ref.shape[1], ccoef_ref.shape[2]
    gx, gy, ma = lax.axis_index("gx"), lax.axis_index("gy"), lax.axis_index("ma")
    me = gx * n_y + gy
    group = n_x * n_y
    has = {
        (-1, 0): gx > 0, (1, 0): gx < n_x - 1, (0, -1): gy > 0, (0, 1): gy < n_y - 1,
    }
    for dx in (-1, 1):
        for dy in (-1, 1):
            has[(dx, dy)] = has[(dx, 0)] & has[(0, dy)]

    def each_peer(action):
        def body(step, carry):
            action(lax.rem(me + step, group))
            return carry

        lax.fori_loop(1, group, body, 0, unroll=group <= 16)

    def lanes_of(j):
        return slice(j * LANES, (j + 1) * LANES)

    own = pl.ds(EDGE, rows)
    spans = [(g, pl.ds(8 * g, min(8, half - 8 * g))) for g in range(cb.shape[3])]
    loads = []

    def load(src, dst):
        loads.append(pltpu.make_async_copy(src, dst, load_sem.at[len(loads)]))
        loads[-1].start()

    load(d_hbm, d_ref)
    for j in range(tiles):
        load(p_hbm.at[:, :, :, pl.ds(j * LANES, LANES)], pv.at[:, :, j, own])
    load(coef_hbm, coef_ref)
    load(ccoef_hbm, ccoef_ref)
    load(r_hbm, r_ref)
    early = len(loads)

    barrier = pltpu.get_barrier_semaphore()
    pl.semaphore_signal(barrier, inc=1, device_id={"ma": 1 - ma}, device_id_type=MESH)
    each_peer(
        lambda k: pl.semaphore_signal(
            barrier, inc=1, device_id={"gx": k // n_y, "gy": k % n_y}, device_id_type=MESH
        )
    )
    for side in (0, 1):
        for level in range(levels):
            for e in range(REACH):
                x = rows - 1 - e if side else e
                for g, span in spans:
                    load(p_hbm.at[span, level, x], cb.at[side, level, REACH + e, g, pl.ds(0, span.size)])

    def zero_if(absent, ref):
        @pl.when(absent)
        def _():
            ref[...] = jnp.zeros_like(ref)

    zero_if(gx == 0, rx_prev)
    zero_if(gx == 0, rc_prev)
    zero_if(gx == n_x - 1, rx_next)
    zero_if(gx == n_x - 1, rc_next)
    rest = -half % 8
    for g, span in spans:
        zero_if(gx == 0, cb.at[0, :, pl.ds(0, REACH), g, pl.ds(0, span.size)])
        zero_if(gx == n_x - 1, cb.at[1, :, pl.ds(0, REACH), g, pl.ds(0, span.size)])
    if rest:
        cb[:, :, :, cb.shape[3] - 1, 8 - rest :] = jnp.zeros((2, levels, 2 * REACH, rest, cols), F32)
    pv[:, :, :, :EDGE] = jnp.zeros((half, levels, tiles, EDGE, LANES), F32)
    pv[:, :, :, EDGE + rows :] = jnp.zeros((half, levels, tiles, EDGE, LANES), F32)
    for side in (0, 1):
        dy = 2 * side - 1
        zero_if(jnp.logical_not(has[(0, dy)]), ry.at[side])
        for way in (0, 1):
            zero_if(jnp.logical_not(has[(2 * way - 1, dy)]), rd.at[side, way])

    moves = []

    def move(src, dst, dx, dy):
        slot = len(moves)
        target = {
            "gx": jnp.clip(gx + dx, 0, n_x - 1) if dx else gx,
            "gy": jnp.clip(gy + dy, 0, n_y - 1) if dy else gy,
        }
        copy = pltpu.make_async_remote_copy(
            src_ref=src, dst_ref=dst, send_sem=send_sem.at[slot], recv_sem=recv_sem.at[slot],
            device_id=target, device_id_type=MESH,
        )
        moves.append((copy, has[(dx, dy)], has[(-dx, -dy)]))

        @pl.when(has[(dx, dy)])
        def _():
            copy.start()

        return slot

    def arrive(slot):
        @pl.when(moves[slot][2])
        def _():
            moves[slot][0].wait_recv()

    def move_rows(level):
        slots_of = []
        for h in range(REACH):
            for g, span in spans:
                for side, x in ((1, h), (0, rows - 1 - h)):
                    dst = cb.at[side, level, h, g, pl.ds(0, span.size)]
                    slots_of.append(move(p_hbm.at[span, level, x], dst, 1 - 2 * side, 0))
        return slots_of

    pl.semaphore_wait(barrier, group)
    e_moves = []
    for k, (src, count) in enumerate(((coef_hbm, 2), (d_hbm, levels))):
        span = pl.ds(2 * k, count)
        e_moves.append(move(src.at[:, pl.ds(0, HALO)], rx_next.at[span], -1, 0))
        e_moves.append(move(src.at[:, pl.ds(rows - HALO, HALO)], rx_prev.at[span], 1, 0))
    row_moves = [move_rows(0)]

    for copy in loads[: 1 + tiles]:
        copy.wait()
    pick = lax.broadcasted_iota(jnp.int32, (cols, ccols), 0) // RATIO
    gather = jnp.where(
        pick == lax.broadcasted_iota(jnp.int32, (cols, ccols), 1), 1.0 / RATIO**2, 0.0
    ).astype(BF16)
    batch = next(k for k in (5, 3, 2, 1) if half % k == 0)

    def restrict(n, carry):
        tall = batch * levels * rows
        values = jnp.concatenate(
            [
                (
                    pv[pl.ds(n * batch, batch), :, j, EDGE : EDGE + rows]
                    * d_ref[:, :, lanes_of(j)][None]
                ).reshape(tall, LANES)
                for j in range(tiles)
            ],
            axis=1,
        )
        line[pl.ds(pl.multiple_of(n * tall, 8), tall)] = split_dot(values, gather)
        return carry

    lax.fori_loop(0, half // batch, restrict, 0)
    count = half * levels * crows
    coarse = line[pl.ds(0, count, stride=RATIO), :]
    for k in range(1, RATIO):
        coarse = coarse + line[pl.ds(k, count, stride=RATIO), :]
    for copy in loads[1 + tiles : early]:
        copy.wait()
    wc[pl.ds(0, half)] = coarse.reshape(half, levels, crows, ccols)
    wc[half] = ccoef_ref[...]
    c_top[...] = wc[:, :, :HALO]
    c_bottom[...] = wc[:, :, crows - HALO :]

    fields = half * levels
    flane = lax.broadcasted_iota(jnp.int32, (rows, LANES), 1)
    clane = lax.broadcasted_iota(jnp.int32, (crows, LANES), 1)
    fl = fr = jnp.zeros((rows, LANES), F32)
    cl = cr = jnp.zeros((crows, LANES), F32)
    for f in range(fields + 2 + levels):
        at = PASSES * f
        if f < fields:
            first = pv[f // levels, f % levels, 0, EDGE : EDGE + rows]
            last = pv[f // levels, f % levels, tiles - 1, EDGE : EDGE + rows]
        elif f < fields + 2:
            first = coef_ref[f - fields, :, :LANES]
            last = coef_ref[f - fields, :, cols - LANES :]
        else:
            first = d_ref[f - fields - 2, :, :LANES]
            last = d_ref[f - fields - 2, :, cols - LANES :]
        fl = jnp.where(flane >= at, pltpu.roll(first, at, 1) if at else first, fl)
        fr = jnp.where(flane >= at, pltpu.roll(last, at + PASSES, 1), fr)
        if f < fields + levels:
            field = wc[f // levels, f % levels]
            cl = jnp.where(
                clane >= at, pltpu.roll(field[:, :LANES], at, 1) if at else field[:, :LANES], cl
            )
            cr = jnp.where(clane >= at, pltpu.roll(field[:, ccols - LANES :], at + PASSES, 1), cr)
    for side, (fine, small) in enumerate(((fl, cl), (fr, cr))):
        strips[side, 0:crows] = small
        strips[side, crows : crows + rows] = fine
        strips[side, crows + rows :] = small
    y_moves = []
    for side in (0, 1):
        dy = 2 * side - 1
        other = 1 - side
        y_moves.append(move(strips.at[side, pl.ds(0, crows + rows)], ry.at[other], 0, dy))
        y_moves.append(move(strips.at[side, pl.ds(0, crows + 8)], rd.at[other, 1], -1, dy))
        y_moves.append(
            move(strips.at[side, pl.ds(crows + rows - 8, crows + 8)], rd.at[other, 0], 1, dy)
        )
    c_moves = [move(c_top, rc_next, -1, 0), move(c_bottom, rc_prev, 1, 0)]
    for level in range(1, levels):
        row_moves.append(move_rows(level))

    lane = lax.broadcasted_iota(jnp.int32, (8, LANES), 1)

    for level in range(levels):
        for j in range(tiles):
            here = d_ref[level, :, lanes_of(j)]
            there = d_ref[level, :, lanes_of((j + 1) % tiles)]
            dv[level, j, :EDGE] = jnp.zeros((EDGE, LANES), F32)
            dv[level, j, EDGE : EDGE + rows] = here
            dv[level, j, EDGE + rows :] = jnp.zeros((EDGE, LANES), F32)
            for k in (1, 2, 3):
                dk[level, k - 1, j] = jnp.where(
                    flane < LANES - k,
                    pltpu.roll(here, LANES - k, 1),
                    pltpu.roll(there, LANES - k, 1),
                )
            for t in range(len(ROWS)):
                ev[level, t, j, :EDGE] = jnp.zeros((EDGE, LANES), F32)
                ev[level, t, j, EDGE + rows :] = jnp.zeros((EDGE, LANES), F32)
    lin = lax.broadcasted_iota(jnp.int32, (LANES, LANES), 0)
    lout = lax.broadcasted_iota(jnp.int32, (LANES, LANES), 1)
    step = lax.rem(lout, PASSES)
    inside = lout < PASSES * fields
    for n, (side, ahead, k) in enumerate(MATRICES):
        if side:
            source = step + (LANES - PASSES if ahead else k - PASSES)
            hit = (lin == source) & (step >= PASSES - k) & inside
        else:
            source = step if ahead else step + (LANES - k)
            hit = (lin == source) & (step < k) & inside
        copies[n] = jnp.where(hit, 1.0, 0.0).astype(BF16)
    period = PASSES * levels
    hit = (lin - PASSES * (fields + 2) == lax.rem(lout, period)) & inside
    copies[COPIES] = jnp.where(hit, 1.0, 0.0).astype(BF16)
    for level in range(levels):
        source = lax.rem(lin, period) - PASSES * level
        for side in (0, 1):
            place = lout - (LANES - PASSES) * side
            hit = (source == place) & (place >= 0) & (place < PASSES) & (lin < PASSES * fields)
            totals[side, :, lanes_of(level)] = jnp.where(hit, 1.0, 0.0).astype(BF16)

    def products(n, carry):
        level = n // (rows // 8)
        at = pl.multiple_of(n % (rows // 8) * 8, 8)
        for j in range(0, tiles, 2):
            total = [[None] * len(PAIRS), [None] * len(PAIRS)]
            for m in range(half):
                here = [pv[m, level, (j + g) % tiles, pl.ds(at + EDGE, 8)] for g in range(3)]
                turned = [[pltpu.roll(v, LANES - k, 1) for v in here] for k in (1, 2, 3)]
                for g in range(2):
                    below = {
                        i: pv[m, level, j + g, pl.ds(at + EDGE + i, 8)] if i else here[g]
                        for i in range(-2, 4)
                    }
                    right = [here[g]] + [
                        jnp.where(lane < LANES - k, turned[k - 1][g], turned[k - 1][g + 1])
                        for k in (1, 2, 3)
                    ]
                    for t, (i, k) in enumerate(PAIRS):
                        v = below[i] * right[k]
                        total[g][t] = v if m == 0 else total[g][t] + v
            for g in range(2):
                for t in range(len(PAIRS)):
                    sums_ref[level, t, pl.ds(at, 8), lanes_of(j + g)] = total[g][t]
        return carry

    lax.fori_loop(0, levels * (rows // 8), products, 0)

    for slot in e_moves:
        arrive(slot)
    for slot in y_moves:
        arrive(slot)

    near = lax.broadcasted_iota(jnp.int32, (8, LANES), 0) < HALO
    for side in (0, 1):
        hyc[side, 0:crows] = ry[side, 0:crows]
        hyc[side, crows : crows + 8] = jnp.where(
            near, rd[side, 1, 0:8], rd[side, 0, crows : crows + 8]
        )
        hv[side, 0:EDGE] = rd[side, 0, 0:8]
        hv[side, EDGE : EDGE + rows] = ry[side, crows : crows + rows]
        hv[side, EDGE + rows :] = rd[side, 1, crows : crows + 8]

    def columns(ref, index, height):
        lane = lax.broadcasted_iota(jnp.int32, (height, LANES), 1)
        at = PASSES * index
        right = pltpu.roll(ref[1], LANES - at, 1)
        left = pltpu.roll(ref[0], LANES - PASSES - at, 1)
        return jnp.where(
            lane < PASSES, right, jnp.where(lane >= LANES - PASSES, left, 0.0)
        )

    def coarse_field(m, level):
        height = crows + 2 * HALO
        tall = jnp.concatenate(
            [wc[m, level], jnp.concatenate([rc_next[m, level], rc_prev[m, level]], axis=0)],
            axis=0,
        )
        return jnp.concatenate([tall, columns(hyc, m * levels + level, height)], axis=1)

    ext_rows, ext_cols = rows + 2 * EDGE, cols + LANES

    def wide(main, index):
        pad = jnp.zeros((EDGE - HALO, cols), F32)
        tall = jnp.concatenate(
            [
                jnp.concatenate([pad, rx_prev[index]], axis=0),
                main,
                jnp.concatenate([rx_next[index], pad], axis=0),
            ],
            axis=0,
        )
        return jnp.concatenate([tall, columns(hv, fields + index, ext_rows)], axis=1)

    ends = [
        value.astype(jnp.int32)
        for value in (has[(-1, 0)], has[(1, 0)], has[(0, -1)], has[(0, 1)])
    ]
    row = lax.broadcasted_iota(jnp.int32, (ext_rows, ext_cols), 0) - EDGE
    col = lax.broadcasted_iota(jnp.int32, (ext_rows, ext_cols), 1)
    outside = (
        ((row < 0) & (ends[0] == 0))
        | ((row >= rows) & (ends[1] == 0))
        | ((col >= cols + LANES // 2) & (ends[2] == 0))
        | ((col >= cols) & (col < cols + LANES // 2) & (ends[3] == 0))
    )
    u = composite(wide(coef_ref[0], 0), wide(coef_ref[1], 1), jnp.where(outside, 0.0, 1.0))

    row = lax.broadcasted_iota(jnp.int32, (rows, cols), 0)
    col = lax.broadcasted_iota(jnp.int32, (rows, cols), 1)
    for t, (i, k) in enumerate(PAIRS):
        if i >= 0:
            value = shifted(u[i, -k], 0, k) if i and k else u[i, k]
            valid = (row < rows - i) & (col < cols - k)
        else:
            value = shifted(u[-i, k], i, 0)
            valid = (row >= -i) & (col < cols - k)
        inner[t] = jnp.where(valid, value[EDGE : EDGE + rows, :cols], 0.0)

    ecol = lax.broadcasted_iota(jnp.int32, (EDGE, cols), 1)
    d_wide = [wide(d_ref[level], 2 + level) for level in range(levels)]
    for side in (0, 1):
        span = slice(rows, rows + 2 * EDGE) if side else slice(0, 2 * EDGE)
        take = slice(0, EDGE) if side else slice(EDGE, 2 * EDGE)
        for n, (i, k) in enumerate(ACROSS):
            move_x = i if side else -i
            if side:
                value = u[i, k][span]
            else:
                value = shifted(u[i, -k][span], move_x, k)
            valid = (ecol + k >= 0) & (ecol + k < cols)
            value = jnp.where(valid, value[take, :cols], 0.0)
            for level in range(levels):
                near_d = shifted(d_wide[level][span], move_x, k)[take, :cols]
                weights[side, level, n] = value * near_d

    edge_sums = []
    for side in (0, 1):
        halo_d = split_dot(hv[side], copies[COPIES])
        weighted = hv[side] * halo_d
        for k in (1, 2, 3):
            away = PASSES - k
            turn = away if side else -away % LANES
            mv[side, k - 1] = pltpu.roll(weighted, turn, 1) if away else weighted
        value = jnp.zeros((rows, LANES), F32)
        for n in range(COPIES):
            which, ahead, k = MATRICES[n]
            if which != side:
                continue
            stack, steps = [], []
            for i in range(k - 3, 4 - k):
                if side and ahead and i >= 0:
                    w = u[i, k][:, cols - LANES : cols]
                elif side and not ahead and i < 0:
                    w = shifted(u[-i, -k][:, cols:], i, 0)
                elif not side and ahead and i > 0:
                    w = u[i, -k][:, :LANES]
                elif not side and not ahead and i <= 0:
                    w = shifted(u[-i, k][:, cols:], i, 0)
                else:
                    continue
                stack.append(w[EDGE : EDGE + rows])
                steps.append(i)
            w = split_dot(jnp.concatenate(stack, axis=0), copies[n])
            for t, i in enumerate(steps):
                value = value + w[t * rows : (t + 1) * rows] * mv[side, k - 1, EDGE + i : EDGE + i + rows]
        value = value * strips[side, crows : crows + rows]
        edge_sums.append(split_dot(value, totals[side]))

    def combine(n, carry):
        level = n // (rows // 8)
        at = pl.multiple_of(n % (rows // 8) * 8, 8)
        for j in range(tiles):
            d_right = [dv[level, j, pl.ds(at + EDGE, 8)]] + [
                dk[level, k - 1, j, pl.ds(at, 8)] for k in (1, 2, 3)
            ]
            d_below = {
                i: dv[level, j, pl.ds(at + EDGE + i, 8)] if i else d_right[0] for i in range(-2, 4)
            }
            up, across = {}, {}
            for t, (i, k) in enumerate(PAIRS):
                value = (
                    inner[t, pl.ds(at, 8), lanes_of(j)]
                    * sums_ref[level, t, pl.ds(at, 8), lanes_of(j)]
                )
                term = value * d_right[k]
                up[i] = up[i] + term if i in up else term
                if i or k:
                    term = value * d_below[i]
                    across[k] = across[k] + term if k in across else term
            acc[level, pl.ds(at, 8), lanes_of(j)] = up[0] + across[0]
            for t, i in enumerate(ROWS):
                ev[level, t, j, pl.ds(at + EDGE, 8)] = up[i]
            for k in (1, 2, 3):
                fv[level, k - 1, j, pl.ds(at, 8)] = across[k]
        return carry

    lax.fori_loop(0, levels * (rows // 8), combine, 0)

    def collect(n, carry):
        level = n // (rows // 8)
        at = pl.multiple_of(n % (rows // 8) * 8, 8)
        turned = [
            [pltpu.roll(fv[level, k - 1, j, pl.ds(at, 8)], k, 1) for j in range(tiles)]
            for k in (1, 2, 3)
        ]
        for j in range(tiles):
            total = acc[level, pl.ds(at, 8), lanes_of(j)]
            for t, i in enumerate(ROWS):
                total = total + ev[level, t, j, pl.ds(at + EDGE - i, 8)]
            for k in (1, 2, 3):
                total = total + jnp.where(lane >= k, turned[k - 1][j], turned[k - 1][j - 1])
            acc[level, pl.ds(at, 8), lanes_of(j)] = total
        return carry

    lax.fori_loop(0, levels * (rows // 8), collect, 0)
    for level in range(levels):
        at = slice(level * LANES, (level + 1) * LANES)
        acc[level, :, :LANES] += edge_sums[0][:, at]
        acc[level, :, cols - LANES :] += edge_sums[1][:, at]

    for slot in c_moves:
        arrive(slot)
    for k, value in enumerate(
        stencil_weights(coarse_field(half, 0), coarse_field(half, 1), crows, ccols, *ends)
    ):
        coarse_weights[k] = value

    def coarse_members(j, carry):
        for i in range(batch):
            m = j * batch + i
            for level in range(levels):
                v = apply_passes(coarse_field(m, level), [coarse_weights.at[k] for k in range(5)])
                line[pl.ds(pl.multiple_of((m * levels + level) * crows, 8), crows)] = v[
                    :crows, :ccols
                ]
        return carry

    lax.fori_loop(0, half // batch, coarse_members, 0)
    spread = jnp.where(
        lax.broadcasted_iota(jnp.int32, (ccols, cols), 1) // RATIO
        == lax.broadcasted_iota(jnp.int32, (ccols, cols), 0),
        1.0, 0.0,
    ).astype(BF16)
    wide_rows = split_dot(line[pl.ds(0, count)], spread)
    for j in range(tiles):
        lanes_out[j] = wide_rows[:, lanes_of(j)]

    upper = lax.broadcasted_iota(jnp.int32, (8, LANES), 0) < RATIO

    def add_coarse(n, carry):
        level, t = n // (rows // 8), n % (rows // 8)
        at = pl.multiple_of(t * 8, 8)
        for j in range(tiles):
            total = None
            for m in range(half):
                base = (m * levels + level) * crows + 2 * t
                a = jnp.broadcast_to(lanes_out[j, pl.ds(base, 1)], (8, LANES))
                b = jnp.broadcast_to(lanes_out[j, pl.ds(base + 1, 1)], (8, LANES))
                v = pv[m, level, j, pl.ds(at + EDGE, 8)] * jnp.where(upper, a, b)
                total = v if m == 0 else total + v
            acc[level, pl.ds(at, 8), lanes_of(j)] += total
        return carry

    lax.fori_loop(0, levels * (rows // 8), add_coarse, 0)

    for copy in loads[early:]:
        copy.wait()
    for level in range(levels):
        for slot in row_moves[level]:
            arrive(slot)
        for side in (0, 1):
            for j in range(tiles):
                total = [None] * REACH
                for g in range(cb.shape[3]):
                    def tile(r, at):
                        return cb[side, level, r, g, :, lanes_of(at % tiles)]

                    halo = {}
                    for h in range(REACH):
                        halo[h, 0] = tile(h, j)
                        for k in range(1, REACH - h):
                            halo[h, k] = jnp.where(
                                lane < LANES - k,
                                pltpu.roll(tile(h, j), LANES - k, 1),
                                pltpu.roll(tile(h, j + 1), LANES - k, 1),
                            )
                            halo[h, -k] = jnp.where(
                                lane >= k,
                                pltpu.roll(tile(h, j), k, 1),
                                pltpu.roll(tile(h, j - 1), k, 1),
                            )
                    for e in range(REACH):
                        x = EDGE - 1 - e if side else e
                        value = None
                        for h in range(REACH - e):
                            i = e + h + 1
                            for k in range(i - 3, 4 - i):
                                w = weights[side, level, ACROSS.index((i, k)), x : x + 1, lanes_of(j)]
                                term = w * halo[h, k]
                                value = term if value is None else value + term
                        value = value * tile(REACH + e, j)
                        total[e] = value if g == 0 else total[e] + value
                for e in range(REACH):
                    x = rows - 1 - e if side else e
                    acc[level, x : x + 1, lanes_of(j)] += jnp.sum(total[e], axis=0, keepdims=True)

    swap = pltpu.make_async_remote_copy(
        src_ref=acc, dst_ref=acc_other, send_sem=send_sem.at[len(moves)],
        recv_sem=recv_sem.at[len(moves)], device_id={"ma": 1 - ma}, device_id_type=MESH,
    )
    swap.start()
    swap.wait_recv()
    d, r = d_ref[...], r_ref[...]
    q = d + (acc[...] + acc_other[...]) / (MEMBERS - 1)
    q_ref[...] = q

    def total_row(value):
        flat = value.reshape(levels * rows // 8, 8, cols)
        tile = jnp.sum(flat, axis=0)
        narrow = tile[:, :LANES]
        for k in range(1, cols // LANES):
            narrow = narrow + tile[:, k * LANES : (k + 1) * LANES]
        return jnp.sum(narrow, axis=0, keepdims=True)

    row = lax.broadcasted_iota(jnp.int32, (8, LANES), 0)
    packed = jnp.zeros((8, LANES), F32)
    for k, value in enumerate((r * r, d * q, r * q, q * q)):
        packed = jnp.where(row == k, total_row(value), packed)
    part[...] = packed
    slots[me] = packed

    def to_peer(k):
        return pltpu.make_async_remote_copy(
            src_ref=part, dst_ref=slots.at[me], send_sem=group_send.at[k],
            recv_sem=group_recv.at[me],
            device_id={"gx": k // n_y, "gy": k % n_y}, device_id_type=MESH,
        )

    def from_peer(k):
        return pltpu.make_async_remote_copy(
            src_ref=part, dst_ref=slots.at[k], send_sem=group_send.at[k],
            recv_sem=group_recv.at[k],
            device_id={"gx": k // n_y, "gy": k % n_y}, device_id_type=MESH,
        )

    each_peer(lambda k: to_peer(k).start())
    swap.wait_send()
    for copy, sends, _ in moves:
        @pl.when(sends)
        def _():
            copy.wait_send()
    each_peer(lambda k: from_peer(k).wait_recv())
    sums = jnp.sum(jnp.sum(slots[...], axis=0), axis=1, keepdims=True)
    norm_old, curvature, cross, image = (sums[k : k + 1] for k in range(4))
    step_length = norm_old / curvature
    norm_new = norm_old + step_length * (step_length * image - 2.0 * cross)
    step_ref[...] = jnp.broadcast_to(step_length, (1, cols))
    growth_ref[...] = jnp.broadcast_to(norm_new / norm_old, (1, cols))
    each_peer(lambda k: to_peer(k).wait_send())


def local(n_x, n_y, perturbations, coefficients, coarse_coefficients, iterate, residual, direction):
    half, levels, rows, cols = perturbations.shape
    _, crows, ccols = coarse_coefficients.shape
    total = half + 1
    group = n_x * n_y
    groups = -(-half // 8)
    n_moves = 4 + 2 * REACH * levels * groups + 6 + 2 + 1
    vmem = pl.BlockSpec(memory_space=pltpu.VMEM)
    q, step_length, growth = pl.pallas_call(
        functools.partial(kernel, (n_x, n_y)),
        out_shape=(
            jax.ShapeDtypeStruct((levels, rows, cols), F32),
            jax.ShapeDtypeStruct((1, cols), F32),
            jax.ShapeDtypeStruct((1, cols), F32),
        ),
        in_specs=[pl.BlockSpec(memory_space=pltpu.HBM)] * 5,
        out_specs=(vmem, vmem, vmem),
        scratch_shapes=[
            pltpu.VMEM((half, levels, cols // LANES, rows + 2 * EDGE, LANES), F32),
            pltpu.VMEM((2, rows, cols), F32),
            pltpu.VMEM((2, crows, ccols), F32),
            pltpu.VMEM((levels, rows, cols), F32),
            pltpu.VMEM((levels, rows, cols), F32),
            pltpu.VMEM((total, levels, crows, ccols), F32),
            pltpu.VMEM((half * levels * rows, ccols), F32),
            pltpu.VMEM((cols // LANES, half * levels * crows, LANES), F32),
            pltpu.VMEM((total, levels, HALO, ccols), F32),
            pltpu.VMEM((total, levels, HALO, ccols), F32),
            pltpu.VMEM((2, rows + 2 * crows, LANES), F32),
            pltpu.VMEM((2 + levels, HALO, cols), F32),
            pltpu.VMEM((2 + levels, HALO, cols), F32),
            pltpu.VMEM((total, levels, HALO, ccols), F32),
            pltpu.VMEM((total, levels, HALO, ccols), F32),
            pltpu.VMEM((2, rows + crows, LANES), F32),
            pltpu.VMEM((2, 2, crows + 8, LANES), F32),
            pltpu.VMEM((2, levels, 2 * REACH, groups, 8, cols), F32),
            pltpu.VMEM((2, rows + 2 * EDGE, LANES), F32),
            pltpu.VMEM((2, crows + 2 * HALO, LANES), F32),
            pltpu.VMEM((levels, len(PAIRS), rows, cols), F32),
            pltpu.VMEM((len(PAIRS), rows, cols), F32),
            pltpu.VMEM((2, levels, len(ACROSS), EDGE, cols), F32),
            pltpu.VMEM((5, crows + 2 * HALO, ccols + LANES), F32),
            pltpu.VMEM((levels, cols // LANES, rows + 2 * EDGE, LANES), F32),
            pltpu.VMEM((levels, 3, cols // LANES, rows, LANES), F32),
            pltpu.VMEM((levels, len(ROWS), cols // LANES, rows + 2 * EDGE, LANES), F32),
            pltpu.VMEM((levels, 3, cols // LANES, rows, LANES), F32),
            pltpu.VMEM((2, 3, rows + 2 * EDGE, LANES), F32),
            pltpu.VMEM((COPIES + 1, LANES, LANES), BF16),
            pltpu.VMEM((2, LANES, levels * LANES), BF16),
            pltpu.VMEM((levels, rows, cols), F32),
            pltpu.VMEM((levels, rows, cols), F32),
            pltpu.VMEM((8, LANES), F32),
            pltpu.VMEM((group, 8, LANES), F32),
            pltpu.SemaphoreType.DMA((4 + cols // LANES + 2 * levels * REACH * groups,)),
            pltpu.SemaphoreType.DMA((n_moves,)),
            pltpu.SemaphoreType.DMA((n_moves,)),
            pltpu.SemaphoreType.DMA((group,)),
            pltpu.SemaphoreType.DMA((group,)),
        ],
        compiler_params=pltpu.CompilerParams(
            collective_id=0, has_side_effects=True, vmem_limit_bytes=62 << 20
        ),
    )(perturbations, coefficients, coarse_coefficients, residual, direction)
    new_iterate = iterate + step_length * direction
    new_residual = residual - step_length * q
    new_direction = new_residual + growth * direction
    return (new_iterate, new_residual, new_direction)


def solution(mesh):
    cell = P(None, "gx", "gy")
    return jax.shard_map(
        functools.partial(local, mesh.shape["gx"], mesh.shape["gy"]),
        mesh=mesh,
        in_specs=(P("ma", None, "gx", "gy"), cell, cell, cell, cell, cell),
        out_specs=(cell, cell, cell),
        check_vma=False,
    )
```

```python
import functools

import jax
import jax.numpy as jnp
from jax import lax
from jax.experimental import pallas as pl
from jax.experimental.pallas import tpu as pltpu
from jax.sharding import PartitionSpec as P

MEMBERS = 30
PASSES = 3
RATIO = 4
HALO = 4
LANES = 128
EDGE = 8
REACH = 3
PAIRS = (
    (0, 0), (0, 1), (0, 2), (0, 3), (1, 0), (2, 0), (3, 0), (1, 1), (1, 2), (2, 1),
    (-1, 1), (-1, 2), (-2, 1),
)
ACROSS = tuple((i, k) for i in (1, 2, 3) for k in range(i - 3, 4 - i))
ROWS = (-2, -1, 1, 2, 3)
MATRICES = tuple((0, True, k) for k in (1, 2)) + tuple((0, False, k) for k in (1, 2, 3))
MATRICES += tuple((1, True, k) for k in (1, 2, 3)) + tuple((1, False, k) for k in (1, 2))
COPIES = len(MATRICES)
MESH = pl.DeviceIdType.MESH
F32 = jnp.float32
BF16 = jnp.bfloat16


def shift_up(u, axis):
    return pltpu.roll(u, u.shape[axis] - 1, axis)


def shift_down(u, axis):
    return pltpu.roll(u, 1, axis)


def split_dot(a, b):
    high = a.astype(BF16)
    low = (a - high.astype(F32)).astype(BF16)
    return jnp.dot(high, b, preferred_element_type=F32) + jnp.dot(
        low, b, preferred_element_type=F32
    )


def stencil_weights(cx, cy, rows, cols, has_prev, has_next, has_left, has_right):
    ext_rows, ext_cols = cx.shape
    row = lax.broadcasted_iota(jnp.int32, (ext_rows, ext_cols), 0)
    col = lax.broadcasted_iota(jnp.int32, (ext_rows, ext_cols), 1)
    outside = (
        ((row >= rows) & (row < rows + HALO) & (has_next == 0))
        | ((row >= rows + HALO) & (has_prev == 0))
        | ((col >= cols) & (col < cols + LANES // 2) & (has_right == 0))
        | ((col >= cols + LANES // 2) & (has_left == 0))
    )
    xp = 0.5 * (cx + shift_up(cx, 0))
    xm = shift_down(xp, 0)
    yp = 0.5 * (cy + shift_up(cy, 1))
    ym = shift_down(yp, 1)
    centre = 1.0 - xp - xm - yp - ym
    return [jnp.where(outside, 0.0, value) for value in (centre, xp, xm, yp, ym)]


def shifted(u, dx, dy):
    if dx:
        u = pltpu.roll(u, -dx % u.shape[0], 0)
    if dy:
        u = pltpu.roll(u, -dy % u.shape[1], 1)
    return u


def composite(cx, cy, inside):
    s = shifted
    half_x = 0.5 * (cx + s(cx, 1, 0))
    half_y = 0.5 * (cy + s(cy, 0, 1))
    d = inside * (1.0 - half_x - s(half_x, -1, 0) - half_y - s(half_y, 0, -1))
    x = inside * s(inside, 1, 0) * half_x
    y = inside * s(inside, 0, 1) * half_y
    x2, y2 = x * x, y * y
    q = x2 + s(x2, -1, 0) + y2 + s(y2, 0, -1)
    dx, dy, dm = s(d, 1, 0), s(d, 0, 1), s(d, 0, -1)
    dxx, dyy, dxy, dxm = s(d, 2, 0), s(d, 0, 2), s(dy, 1, 0), s(dm, 1, 0)
    xx1, xy1, xm1 = s(x, 1, 0), s(x, 0, 1), s(x, 0, -1)
    yx1, yy1, ym = s(y, 1, 0), s(y, 0, 1), s(y, 0, -1)
    ymx = s(ym, 1, 0)
    xx, yy, xy, yx = x * xx1, y * yy1, x * yx1, y * xy1
    xym, ymx_then, ymym = x * ymx, ym * xm1, s(yy, 0, -2)
    u = {}
    u[0, 0] = d * (d * d + 2.0 * q) + x2 * dx + s(x2 * d, -1, 0) + y2 * dy + s(y2 * d, 0, -1)
    u[1, 0] = x * (d * d + d * dx + dx * dx + q + s(q, 1, 0) - x2) + yx * yx1 + ymx_then * ymx
    u[0, 1] = y * (d * d + d * dy + dy * dy + q + s(q, 0, 1) - y2) + xy * xy1 + s(x * yx, -1, 0)
    u[2, 0] = xx * (d + dx + dxx)
    u[0, 2] = yy * (d + dy + dyy)
    u[3, 0] = xx * s(x, 2, 0)
    u[0, 3] = yy * s(y, 0, 2)
    u[1, 1] = xy * (d + dx + dxy) + yx * (d + dy + dxy)
    u[1, -1] = xym * (d + dx + dxm) + ymx_then * (d + dm + dxm)
    u[2, 1] = xx * s(y, 2, 0) + x * s(yx, 1, 0) + y * s(xx, 0, 1)
    u[2, -1] = xx * s(ymx, 1, 0) + x * s(ymx_then, 1, 0) + ym * s(xx, 0, -1)
    u[1, 2] = x * s(yy, 1, 0) + y * s(xy, 0, 1) + yy * s(x, 0, 2)
    u[1, -2] = x * s(ymym, 1, 0) + ym * s(xym, 0, -1) + ymym * s(x, 0, -2)
    return u


def kernel(
    sizes,
    p_hbm, coef_hbm, ccoef_hbm, r_hbm, d_hbm,
    q_ref, step_ref, growth_ref,
    pv, coef_ref, ccoef_ref, r_ref, d_ref,
    wct, wch, line, lanes_out, packs, packs_y, packs_d, strips,
    rx_next, rx_prev, rc_next, rc_prev, ry, rd,
    cb, hv, hyc, sums_ref, inner, weights, coarse_weights, dv, dk, ev, fv, mv, copies, totals,
    acc, acc_other, part, slots,
    load_sem, send_sem, recv_sem, group_send, group_recv,
):
    n_x, n_y = sizes
    levels, rows, cols = d_ref.shape
    half, tiles = pv.shape[0], cols // LANES
    crows, ccols = ccoef_ref.shape[1], ccoef_ref.shape[2]
    gx, gy, ma = lax.axis_index("gx"), lax.axis_index("gy"), lax.axis_index("ma")
    me = gx * n_y + gy
    group = n_x * n_y
    has = {
        (-1, 0): gx > 0, (1, 0): gx < n_x - 1, (0, -1): gy > 0, (0, 1): gy < n_y - 1,
    }
    for dx in (-1, 1):
        for dy in (-1, 1):
            has[(dx, dy)] = has[(dx, 0)] & has[(0, dy)]

    def each_peer(action):
        def body(step, carry):
            action(lax.rem(me + step, group))
            return carry

        lax.fori_loop(1, group, body, 0, unroll=group <= 16)

    def lanes_of(j):
        return slice(j * LANES, (j + 1) * LANES)

    own = pl.ds(EDGE, rows)
    fields = half * levels
    bands = wct.shape[1]
    spans = [(g, pl.ds(8 * g, min(8, half - 8 * g))) for g in range(cb.shape[3])]
    loads = []

    def load(src, dst):
        loads.append(pltpu.make_async_copy(src, dst, load_sem.at[len(loads)]))
        loads[-1].start()

    load(d_hbm, d_ref)
    for j in range(tiles):
        load(p_hbm.at[:, :, :, pl.ds(j * LANES, LANES)], pv.at[:, :, j, own])
    load(coef_hbm, coef_ref)
    load(ccoef_hbm, ccoef_ref)
    load(r_hbm, r_ref)
    early = len(loads)

    barrier = pltpu.get_barrier_semaphore()
    pl.semaphore_signal(barrier, inc=1, device_id={"ma": 1 - ma}, device_id_type=MESH)
    each_peer(
        lambda k: pl.semaphore_signal(
            barrier, inc=1, device_id={"gx": k // n_y, "gy": k % n_y}, device_id_type=MESH
        )
    )
    for side in (0, 1):
        for level in range(levels):
            for e in range(REACH):
                x = rows - 1 - e if side else e
                for g, span in spans:
                    load(p_hbm.at[span, level, x], cb.at[side, level, REACH + e, g, pl.ds(0, span.size)])

    def zero_if(absent, ref):
        @pl.when(absent)
        def _():
            ref[...] = jnp.zeros_like(ref)

    zero_if(gx == 0, rx_prev)
    zero_if(gx == 0, rc_prev)
    zero_if(gx == n_x - 1, rx_next)
    zero_if(gx == n_x - 1, rc_next)
    rest = -half % 8
    for g, span in spans:
        zero_if(gx == 0, cb.at[0, :, pl.ds(0, REACH), g, pl.ds(0, span.size)])
        zero_if(gx == n_x - 1, cb.at[1, :, pl.ds(0, REACH), g, pl.ds(0, span.size)])
    if rest:
        cb[:, :, :, cb.shape[3] - 1, 8 - rest :] = jnp.zeros((2, levels, 2 * REACH, rest, cols), F32)
    pv[:, :, :, :EDGE] = jnp.zeros((half, levels, tiles, EDGE, LANES), F32)
    pv[:, :, :, EDGE + rows :] = jnp.zeros((half, levels, tiles, EDGE, LANES), F32)
    zero_if(gx == 0, wct.at[pl.ds(HALO - REACH, REACH)])
    zero_if(gx == n_x - 1, wct.at[pl.ds(HALO + crows, REACH)])
    for x in (0, 2 * HALO + crows - 1):
        wct[x] = jnp.zeros((bands, 8, LANES), F32)
    for f in range(fields, 8 * bands):
        line[f * rows : (f + 1) * rows] = jnp.zeros((rows, ccols), F32)
    for side in (0, 1):
        dy = 2 * side - 1
        zero_if(jnp.logical_not(has[(0, dy)]), ry.at[side])
        zero_if(jnp.logical_not(has[(0, dy)]), packs_y.at[side])
        for way in (0, 1):
            zero_if(jnp.logical_not(has[(2 * way - 1, dy)]), rd.at[side, way])
            zero_if(jnp.logical_not(has[(2 * way - 1, dy)]), packs_d.at[side, way])

    moves = []

    def move(src, dst, dx, dy):
        slot = len(moves)
        target = {
            "gx": jnp.clip(gx + dx, 0, n_x - 1) if dx else gx,
            "gy": jnp.clip(gy + dy, 0, n_y - 1) if dy else gy,
        }
        copy = pltpu.make_async_remote_copy(
            src_ref=src, dst_ref=dst, send_sem=send_sem.at[slot], recv_sem=recv_sem.at[slot],
            device_id=target, device_id_type=MESH,
        )
        moves.append((copy, has[(dx, dy)], has[(-dx, -dy)]))

        @pl.when(has[(dx, dy)])
        def _():
            copy.start()

        return slot

    def arrive(slot):
        @pl.when(moves[slot][2])
        def _():
            moves[slot][0].wait_recv()

    def move_rows(level):
        slots_of = []
        for h in range(REACH):
            for g, span in spans:
                for side, x in ((1, h), (0, rows - 1 - h)):
                    dst = cb.at[side, level, h, g, pl.ds(0, span.size)]
                    slots_of.append(move(p_hbm.at[span, level, x], dst, 1 - 2 * side, 0))
        return slots_of

    pl.semaphore_wait(barrier, group)
    e_moves = []
    for k, (src, count) in enumerate(((coef_hbm, 2), (d_hbm, levels))):
        span = pl.ds(2 * k, count)
        e_moves.append(move(src.at[:, pl.ds(0, HALO)], rx_next.at[span], -1, 0))
        e_moves.append(move(src.at[:, pl.ds(rows - HALO, HALO)], rx_prev.at[span], 1, 0))
    e_moves.append(move(ccoef_hbm.at[:, pl.ds(0, HALO)], rc_next, -1, 0))
    e_moves.append(move(ccoef_hbm.at[:, pl.ds(crows - HALO, HALO)], rc_prev, 1, 0))
    row_moves = [move_rows(0)]

    for copy in loads[: 1 + tiles]:
        copy.wait()
    pick = lax.broadcasted_iota(jnp.int32, (cols, ccols), 0) // RATIO
    gather = jnp.where(
        pick == lax.broadcasted_iota(jnp.int32, (cols, ccols), 1), 1.0 / RATIO**2, 0.0
    ).astype(BF16)
    batch = next(k for k in (5, 3, 2, 1) if half % k == 0)

    def restrict(n, carry):
        tall = batch * levels * rows
        values = jnp.concatenate(
            [
                (
                    pv[pl.ds(n * batch, batch), :, j, EDGE : EDGE + rows]
                    * d_ref[:, :, lanes_of(j)][None]
                ).reshape(tall, LANES)
                for j in range(tiles)
            ],
            axis=1,
        )
        line[pl.ds(pl.multiple_of(n * tall, 8), tall)] = split_dot(values, gather)
        return carry

    lax.fori_loop(0, half // batch, restrict, 0)
    for copy in loads[1 + tiles : early]:
        copy.wait()
    for x in range(crows):
        for g in range(bands):
            value = None
            for k in range(RATIO):
                term = line[pl.ds(g * 8 * rows + RATIO * x + k, 8, stride=rows), :]
                value = term if k == 0 else value + term
            wct[HALO + x, g] = value

    flane = lax.broadcasted_iota(jnp.int32, (rows, LANES), 1)
    clane = lax.broadcasted_iota(jnp.int32, (crows, LANES), 1)
    fl = fr = jnp.zeros((rows, LANES), F32)
    cl = cr = jnp.zeros((crows, LANES), F32)
    for f in (0, 1):
        at = PASSES * f
        field = ccoef_ref[f]
        cl = jnp.where(
            clane >= at, pltpu.roll(field[:, :LANES], at, 1) if at else field[:, :LANES], cl
        )
        cr = jnp.where(clane >= at, pltpu.roll(field[:, ccols - LANES :], at + PASSES, 1), cr)
    for f in range(fields + 2 + levels):
        at = PASSES * f
        if f < fields:
            first = pv[f // levels, f % levels, 0, EDGE : EDGE + rows]
            last = pv[f // levels, f % levels, tiles - 1, EDGE : EDGE + rows]
        elif f < fields + 2:
            first = coef_ref[f - fields, :, :LANES]
            last = coef_ref[f - fields, :, cols - LANES :]
        else:
            first = d_ref[f - fields - 2, :, :LANES]
            last = d_ref[f - fields - 2, :, cols - LANES :]
        fl = jnp.where(flane >= at, pltpu.roll(first, at, 1) if at else first, fl)
        fr = jnp.where(flane >= at, pltpu.roll(last, at + PASSES, 1), fr)
    for side, (fine, small) in enumerate(((fl, cl), (fr, cr))):
        strips[side, 0:crows] = small
        strips[side, crows : crows + rows] = fine
        strips[side, crows + rows :] = small
    blane = lax.broadcasted_iota(jnp.int32, (8, LANES), 1)
    for g in range(bands):
        for side in (0, 1):
            value = jnp.zeros((8, LANES), F32)
            for x in range(crows):
                at = PASSES * x
                turn = at + PASSES * side
                field = wct[HALO + x, g]
                value = jnp.where(blane >= at, pltpu.roll(field, turn, 1) if turn else field, value)
            packs[side, g] = value
    y_moves = []
    for side in (0, 1):
        dy = 2 * side - 1
        other = 1 - side
        y_moves.append(move(strips.at[side, pl.ds(0, crows + rows)], ry.at[other], 0, dy))
        y_moves.append(move(strips.at[side, pl.ds(0, crows + 8)], rd.at[other, 1], -1, dy))
        y_moves.append(
            move(strips.at[side, pl.ds(crows + rows - 8, crows + 8)], rd.at[other, 0], 1, dy)
        )
    c_moves = []
    for side in (0, 1):
        dy = 2 * side - 1
        c_moves.append(move(packs.at[side], packs_y.at[1 - side], 0, dy))
        c_moves.append(move(packs.at[side], packs_d.at[1 - side, 1], -1, dy))
        c_moves.append(move(packs.at[side], packs_d.at[1 - side, 0], 1, dy))
    c_moves.append(
        move(wct.at[pl.ds(HALO, REACH)], wct.at[pl.ds(HALO + crows, REACH)], -1, 0)
    )
    c_moves.append(
        move(wct.at[pl.ds(HALO + crows - REACH, REACH)], wct.at[pl.ds(HALO - REACH, REACH)], 1, 0)
    )
    for level in range(1, levels):
        row_moves.append(move_rows(level))

    lane = blane
    for level in range(levels):
        for j in range(tiles):
            here = d_ref[level, :, lanes_of(j)]
            there = d_ref[level, :, lanes_of((j + 1) % tiles)]
            dv[level, j, :EDGE] = jnp.zeros((EDGE, LANES), F32)
            dv[level, j, EDGE : EDGE + rows] = here
            dv[level, j, EDGE + rows :] = jnp.zeros((EDGE, LANES), F32)
            for k in (1, 2, 3):
                dk[level, k - 1, j] = jnp.where(
                    flane < LANES - k,
                    pltpu.roll(here, LANES - k, 1),
                    pltpu.roll(there, LANES - k, 1),
                )
            for t in range(len(ROWS)):
                ev[level, t, j, :EDGE] = jnp.zeros((EDGE, LANES), F32)
                ev[level, t, j, EDGE + rows :] = jnp.zeros((EDGE, LANES), F32)
    lin = lax.broadcasted_iota(jnp.int32, (LANES, LANES), 0)
    lout = lax.broadcasted_iota(jnp.int32, (LANES, LANES), 1)
    step = lax.rem(lout, PASSES)
    inside = lout < PASSES * fields
    for n, (side, ahead, k) in enumerate(MATRICES):
        if side:
            source = step + (LANES - PASSES if ahead else k - PASSES)
            hit = (lin == source) & (step >= PASSES - k) & inside
        else:
            source = step if ahead else step + (LANES - k)
            hit = (lin == source) & (step < k) & inside
        copies[n] = jnp.where(hit, 1.0, 0.0).astype(BF16)
    period = PASSES * levels
    hit = (lin - PASSES * (fields + 2) == lax.rem(lout, period)) & inside
    copies[COPIES] = jnp.where(hit, 1.0, 0.0).astype(BF16)
    for level in range(levels):
        source = lax.rem(lin, period) - PASSES * level
        for side in (0, 1):
            place = lout - (LANES - PASSES) * side
            hit = (source == place) & (place >= 0) & (place < PASSES) & (lin < PASSES * fields)
            totals[side, :, lanes_of(level)] = jnp.where(hit, 1.0, 0.0).astype(BF16)

    def products(n, carry):
        level = n // (rows // 8)
        at = pl.multiple_of(n % (rows // 8) * 8, 8)
        for j in range(0, tiles, 2):
            total = [[None] * len(PAIRS), [None] * len(PAIRS)]
            for m in range(half):
                here = [pv[m, level, (j + g) % tiles, pl.ds(at + EDGE, 8)] for g in range(3)]
                turned = [[pltpu.roll(v, LANES - k, 1) for v in here] for k in (1, 2, 3)]
                for g in range(2):
                    below = {
                        i: pv[m, level, j + g, pl.ds(at + EDGE + i, 8)] if i else here[g]
                        for i in range(-2, 4)
                    }
                    right = [here[g]] + [
                        jnp.where(lane < LANES - k, turned[k - 1][g], turned[k - 1][g + 1])
                        for k in (1, 2, 3)
                    ]
                    for t, (i, k) in enumerate(PAIRS):
                        v = below[i] * right[k]
                        total[g][t] = v if m == 0 else total[g][t] + v
            for g in range(2):
                for t in range(len(PAIRS)):
                    sums_ref[level, t, pl.ds(at, 8), lanes_of(j + g)] = total[g][t]
        return carry

    lax.fori_loop(0, levels * (rows // 8), products, 0)

    for slot in e_moves:
        arrive(slot)
    for slot in y_moves:
        arrive(slot)

    near = lax.broadcasted_iota(jnp.int32, (8, LANES), 0) < HALO
    for side in (0, 1):
        hyc[side, 0:crows] = ry[side, 0:crows]
        hyc[side, crows : crows + 8] = jnp.where(
            near, rd[side, 1, 0:8], rd[side, 0, crows : crows + 8]
        )
        hv[side, 0:EDGE] = rd[side, 0, 0:8]
        hv[side, EDGE : EDGE + rows] = ry[side, crows : crows + rows]
        hv[side, EDGE + rows :] = rd[side, 1, crows : crows + 8]

    def columns(ref, index, height):
        lane = lax.broadcasted_iota(jnp.int32, (height, LANES), 1)
        at = PASSES * index
        right = pltpu.roll(ref[1], LANES - at, 1)
        left = pltpu.roll(ref[0], LANES - PASSES - at, 1)
        return jnp.where(
            lane < PASSES, right, jnp.where(lane >= LANES - PASSES, left, 0.0)
        )

    def coarse_field(f):
        height = crows + 2 * HALO
        tall = jnp.concatenate(
            [ccoef_ref[f], jnp.concatenate([rc_next[f], rc_prev[f]], axis=0)], axis=0
        )
        return jnp.concatenate([tall, columns(hyc, f, height)], axis=1)

    ext_rows, ext_cols = rows + 2 * EDGE, cols + LANES

    def wide(main, index):
        pad = jnp.zeros((EDGE - HALO, cols), F32)
        tall = jnp.concatenate(
            [
                jnp.concatenate([pad, rx_prev[index]], axis=0),
                main,
                jnp.concatenate([rx_next[index], pad], axis=0),
            ],
            axis=0,
        )
        return jnp.concatenate([tall, columns(hv, fields + index, ext_rows)], axis=1)

    ends = [
        value.astype(jnp.int32)
        for value in (has[(-1, 0)], has[(1, 0)], has[(0, -1)], has[(0, 1)])
    ]
    row = lax.broadcasted_iota(jnp.int32, (ext_rows, ext_cols), 0) - EDGE
    col = lax.broadcasted_iota(jnp.int32, (ext_rows, ext_cols), 1)
    outside = (
        ((row < 0) & (ends[0] == 0))
        | ((row >= rows) & (ends[1] == 0))
        | ((col >= cols + LANES // 2) & (ends[2] == 0))
        | ((col >= cols) & (col < cols + LANES // 2) & (ends[3] == 0))
    )
    u = composite(wide(coef_ref[0], 0), wide(coef_ref[1], 1), jnp.where(outside, 0.0, 1.0))

    row = lax.broadcasted_iota(jnp.int32, (rows, cols), 0)
    col = lax.broadcasted_iota(jnp.int32, (rows, cols), 1)
    for t, (i, k) in enumerate(PAIRS):
        if i >= 0:
            value = shifted(u[i, -k], 0, k) if i and k else u[i, k]
            valid = (row < rows - i) & (col < cols - k)
        else:
            value = shifted(u[-i, k], i, 0)
            valid = (row >= -i) & (col < cols - k)
        inner[t] = jnp.where(valid, value[EDGE : EDGE + rows, :cols], 0.0)

    ecol = lax.broadcasted_iota(jnp.int32, (EDGE, cols), 1)
    d_wide = [wide(d_ref[level], 2 + level) for level in range(levels)]
    for side in (0, 1):
        span = slice(rows, rows + 2 * EDGE) if side else slice(0, 2 * EDGE)
        take = slice(0, EDGE) if side else slice(EDGE, 2 * EDGE)
        for n, (i, k) in enumerate(ACROSS):
            move_x = i if side else -i
            if side:
                value = u[i, k][span]
            else:
                value = shifted(u[i, -k][span], move_x, k)
            valid = (ecol + k >= 0) & (ecol + k < cols)
            value = jnp.where(valid, value[take, :cols], 0.0)
            for level in range(levels):
                near_d = shifted(d_wide[level][span], move_x, k)[take, :cols]
                weights[side, level, n] = value * near_d

    edge_sums = []
    for side in (0, 1):
        halo_d = split_dot(hv[side], copies[COPIES])
        weighted = hv[side] * halo_d
        for k in (1, 2, 3):
            away = PASSES - k
            turn = away if side else -away % LANES
            mv[side, k - 1] = pltpu.roll(weighted, turn, 1) if away else weighted
        value = jnp.zeros((rows, LANES), F32)
        for n in range(COPIES):
            which, ahead, k = MATRICES[n]
            if which != side:
                continue
            stack, steps = [], []
            for i in range(k - 3, 4 - k):
                if side and ahead and i >= 0:
                    w = u[i, k][:, cols - LANES : cols]
                elif side and not ahead and i < 0:
                    w = shifted(u[-i, -k][:, cols:], i, 0)
                elif not side and ahead and i > 0:
                    w = u[i, -k][:, :LANES]
                elif not side and not ahead and i <= 0:
                    w = shifted(u[-i, k][:, cols:], i, 0)
                else:
                    continue
                stack.append(w[EDGE : EDGE + rows])
                steps.append(i)
            w = split_dot(jnp.concatenate(stack, axis=0), copies[n])
            for t, i in enumerate(steps):
                value = value + w[t * rows : (t + 1) * rows] * mv[side, k - 1, EDGE + i : EDGE + i + rows]
        value = value * strips[side, crows : crows + rows]
        edge_sums.append(split_dot(value, totals[side]))

    def combine(n, carry):
        level = n // (rows // 8)
        at = pl.multiple_of(n % (rows // 8) * 8, 8)
        for j in range(tiles):
            d_right = [dv[level, j, pl.ds(at + EDGE, 8)]] + [
                dk[level, k - 1, j, pl.ds(at, 8)] for k in (1, 2, 3)
            ]
            d_below = {
                i: dv[level, j, pl.ds(at + EDGE + i, 8)] if i else d_right[0] for i in range(-2, 4)
            }
            up, across = {}, {}
            for t, (i, k) in enumerate(PAIRS):
                value = (
                    inner[t, pl.ds(at, 8), lanes_of(j)]
                    * sums_ref[level, t, pl.ds(at, 8), lanes_of(j)]
                )
                term = value * d_right[k]
                up[i] = up[i] + term if i in up else term
                if i or k:
                    term = value * d_below[i]
                    across[k] = across[k] + term if k in across else term
            acc[level, pl.ds(at, 8), lanes_of(j)] = up[0] + across[0]
            for t, i in enumerate(ROWS):
                ev[level, t, j, pl.ds(at + EDGE, 8)] = up[i]
            for k in (1, 2, 3):
                fv[level, k - 1, j, pl.ds(at, 8)] = across[k]
        return carry

    lax.fori_loop(0, levels * (rows // 8), combine, 0, unroll=2)

    def collect(n, carry):
        level = n // (rows // 8)
        at = pl.multiple_of(n % (rows // 8) * 8, 8)
        turned = [
            [pltpu.roll(fv[level, k - 1, j, pl.ds(at, 8)], k, 1) for j in range(tiles)]
            for k in (1, 2, 3)
        ]
        for j in range(tiles):
            total = acc[level, pl.ds(at, 8), lanes_of(j)]
            for t, i in enumerate(ROWS):
                total = total + ev[level, t, j, pl.ds(at + EDGE - i, 8)]
            for k in (1, 2, 3):
                total = total + jnp.where(lane >= k, turned[k - 1][j], turned[k - 1][j - 1])
            acc[level, pl.ds(at, 8), lanes_of(j)] = total
        return carry

    lax.fori_loop(0, levels * (rows // 8), collect, 0, unroll=2)
    for level in range(levels):
        at = slice(level * LANES, (level + 1) * LANES)
        acc[level, :, :LANES] += edge_sums[0][:, at]
        acc[level, :, cols - LANES :] += edge_sums[1][:, at]

    for slot in c_moves:
        arrive(slot)
    for k, value in enumerate(
        stencil_weights(coarse_field(0), coarse_field(1), crows, ccols, *ends)
    ):
        coarse_weights[k] = value
    for x in range(-REACH, crows + REACH):
        for g in range(bands):
            way = 0 if x < 0 else 1
            inner_row = 0 <= x < crows
            left = packs_y[0, g] if inner_row else packs_d[0, way, g]
            right = packs_y[1, g] if inner_row else packs_d[1, way, g]
            at = PASSES * (x % crows)
            if at:
                right = pltpu.roll(right, LANES - at, 1)
            left = pltpu.roll(left, LANES - PASSES - at, 1)
            wch[0, HALO + x, g] = jnp.where(
                blane < PASSES, right, jnp.where(blane >= LANES - PASSES, left, 0.0)
            )
    for step in range(PASSES):
        low = HALO - REACH + 1 + step
        source = [wct, wch.at[0]] if step == 0 else [wch.at[2 * step - 1], wch.at[2 * step]]
        last = step == PASSES - 1

        def coarse_row(x, carry):
            w = [
                [coarse_weights[k, pl.ds((x + crows + HALO) % (crows + 2 * HALO), 1),
                                lanes_of(q)] for k in range(5)]
                for q in range(1 if last else 2)
            ]
            for g in range(bands):
                here = [source[q][x, g] for q in (0, 1)]
                ahead = [pltpu.roll(v, LANES - 1, 1) for v in here]
                back = [pltpu.roll(v, 1, 1) for v in here]
                for q in range(1 if last else 2):
                    value = (
                        w[q][0] * here[q]
                        + w[q][1] * source[q][x + 1, g]
                        + w[q][2] * source[q][x - 1, g]
                        + w[q][3] * jnp.where(blane < LANES - 1, ahead[q], ahead[1 - q])
                        + w[q][4] * jnp.where(blane >= 1, back[q], back[1 - q])
                    )
                    if last:
                        at = pl.multiple_of(((x - HALO) * bands + g) * 8, 8)
                        line[pl.ds(at, 8)] = value
                    else:
                        wch[2 * step + 1 + q, x, g] = value
            return carry

        for x in range(low, crows + 2 * HALO - low):
            coarse_row(x, 0)
    spread = jnp.where(
        lax.broadcasted_iota(jnp.int32, (ccols, cols), 1) // RATIO
        == lax.broadcasted_iota(jnp.int32, (ccols, cols), 0),
        1.0, 0.0,
    ).astype(BF16)
    wide_rows = split_dot(line[pl.ds(0, crows * bands * 8)], spread)
    for j in range(tiles):
        lanes_out[j] = wide_rows[:, lanes_of(j)]

    upper = lax.broadcasted_iota(jnp.int32, (8, LANES), 0) < RATIO

    def add_coarse(n, carry):
        level, t = n // (rows // 8), n % (rows // 8)
        at = pl.multiple_of(t * 8, 8)
        for j in range(tiles):
            total = None
            for m in range(half):
                base = 2 * t * (8 * bands) + m * levels + level
                a = jnp.broadcast_to(lanes_out[j, pl.ds(base, 1)], (8, LANES))
                b = jnp.broadcast_to(lanes_out[j, pl.ds(base + 8 * bands, 1)], (8, LANES))
                v = pv[m, level, j, pl.ds(at + EDGE, 8)] * jnp.where(upper, a, b)
                total = v if m == 0 else total + v
            acc[level, pl.ds(at, 8), lanes_of(j)] += total
        return carry

    lax.fori_loop(0, levels * (rows // 8), add_coarse, 0)

    for copy in loads[early:]:
        copy.wait()
    for level in range(levels):
        for slot in row_moves[level]:
            arrive(slot)
        for side in (0, 1):
            for j in range(tiles):
                total = [None] * REACH
                for g in range(cb.shape[3]):
                    def tile(r, at):
                        return cb[side, level, r, g, :, lanes_of(at % tiles)]

                    halo = {}
                    for h in range(REACH):
                        halo[h, 0] = tile(h, j)
                        for k in range(1, REACH - h):
                            halo[h, k] = jnp.where(
                                lane < LANES - k,
                                pltpu.roll(tile(h, j), LANES - k, 1),
                                pltpu.roll(tile(h, j + 1), LANES - k, 1),
                            )
                            halo[h, -k] = jnp.where(
                                lane >= k,
                                pltpu.roll(tile(h, j), k, 1),
                                pltpu.roll(tile(h, j - 1), k, 1),
                            )
                    for e in range(REACH):
                        x = EDGE - 1 - e if side else e
                        value = None
                        for h in range(REACH - e):
                            i = e + h + 1
                            for k in range(i - 3, 4 - i):
                                w = weights[side, level, ACROSS.index((i, k)), x : x + 1, lanes_of(j)]
                                term = w * halo[h, k]
                                value = term if value is None else value + term
                        value = value * tile(REACH + e, j)
                        total[e] = value if g == 0 else total[e] + value
                for e in range(REACH):
                    x = rows - 1 - e if side else e
                    acc[level, x : x + 1, lanes_of(j)] += jnp.sum(total[e], axis=0, keepdims=True)

    swap = pltpu.make_async_remote_copy(
        src_ref=acc, dst_ref=acc_other, send_sem=send_sem.at[len(moves)],
        recv_sem=recv_sem.at[len(moves)], device_id={"ma": 1 - ma}, device_id_type=MESH,
    )
    swap.start()
    swap.wait_recv()
    d, r = d_ref[...], r_ref[...]
    q = d + (acc[...] + acc_other[...]) / (MEMBERS - 1)
    q_ref[...] = q

    def total_row(value):
        flat = value.reshape(levels * rows // 8, 8, cols)
        tile = jnp.sum(flat, axis=0)
        narrow = tile[:, :LANES]
        for k in range(1, cols // LANES):
            narrow = narrow + tile[:, k * LANES : (k + 1) * LANES]
        return jnp.sum(narrow, axis=0, keepdims=True)

    row = lax.broadcasted_iota(jnp.int32, (8, LANES), 0)
    packed = jnp.zeros((8, LANES), F32)
    for k, value in enumerate((r * r, d * q, r * q, q * q)):
        packed = jnp.where(row == k, total_row(value), packed)
    part[...] = packed
    slots[me] = packed

    def to_peer(k):
        return pltpu.make_async_remote_copy(
            src_ref=part, dst_ref=slots.at[me], send_sem=group_send.at[k],
            recv_sem=group_recv.at[me],
            device_id={"gx": k // n_y, "gy": k % n_y}, device_id_type=MESH,
        )

    def from_peer(k):
        return pltpu.make_async_remote_copy(
            src_ref=part, dst_ref=slots.at[k], send_sem=group_send.at[k],
            recv_sem=group_recv.at[k],
            device_id={"gx": k // n_y, "gy": k % n_y}, device_id_type=MESH,
        )

    each_peer(lambda k: to_peer(k).start())
    swap.wait_send()
    for copy, sends, _ in moves:
        @pl.when(sends)
        def _():
            copy.wait_send()
    each_peer(lambda k: from_peer(k).wait_recv())
    sums = jnp.sum(jnp.sum(slots[...], axis=0), axis=1, keepdims=True)
    norm_old, curvature, cross, image = (sums[k : k + 1] for k in range(4))
    step_length = norm_old / curvature
    norm_new = norm_old + step_length * (step_length * image - 2.0 * cross)
    step_ref[...] = jnp.broadcast_to(step_length, (1, cols))
    growth_ref[...] = jnp.broadcast_to(norm_new / norm_old, (1, cols))
    each_peer(lambda k: to_peer(k).wait_send())


def local(n_x, n_y, perturbations, coefficients, coarse_coefficients, iterate, residual, direction):
    half, levels, rows, cols = perturbations.shape
    _, crows, ccols = coarse_coefficients.shape
    group = n_x * n_y
    groups = -(-half // 8)
    bands = -(-half * levels // 8)
    n_moves = 6 + 2 * REACH * levels * groups + 6 + 8 + 1
    vmem = pl.BlockSpec(memory_space=pltpu.VMEM)
    q, step_length, growth = pl.pallas_call(
        functools.partial(kernel, (n_x, n_y)),
        out_shape=(
            jax.ShapeDtypeStruct((levels, rows, cols), F32),
            jax.ShapeDtypeStruct((1, cols), F32),
            jax.ShapeDtypeStruct((1, cols), F32),
        ),
        in_specs=[pl.BlockSpec(memory_space=pltpu.HBM)] * 5,
        out_specs=(vmem, vmem, vmem),
        scratch_shapes=[
            pltpu.VMEM((half, levels, cols // LANES, rows + 2 * EDGE, LANES), F32),
            pltpu.VMEM((2, rows, cols), F32),
            pltpu.VMEM((2, crows, ccols), F32),
            pltpu.VMEM((levels, rows, cols), F32),
            pltpu.VMEM((levels, rows, cols), F32),
            pltpu.VMEM((crows + 2 * HALO, bands, 8, LANES), F32),
            pltpu.VMEM((2 * PASSES - 1, crows + 2 * HALO, bands, 8, LANES), F32),
            pltpu.VMEM((8 * bands * rows, ccols), F32),
            pltpu.VMEM((cols // LANES, 8 * bands * crows, LANES), F32),
            pltpu.VMEM((2, bands, 8, LANES), F32),
            pltpu.VMEM((2, bands, 8, LANES), F32),
            pltpu.VMEM((2, 2, bands, 8, LANES), F32),
            pltpu.VMEM((2, rows + 2 * crows, LANES), F32),
            pltpu.VMEM((2 + levels, HALO, cols), F32),
            pltpu.VMEM((2 + levels, HALO, cols), F32),
            pltpu.VMEM((2, HALO, ccols), F32),
            pltpu.VMEM((2, HALO, ccols), F32),
            pltpu.VMEM((2, rows + crows, LANES), F32),
            pltpu.VMEM((2, 2, crows + 8, LANES), F32),
            pltpu.VMEM((2, levels, 2 * REACH, groups, 8, cols), F32),
            pltpu.VMEM((2, rows + 2 * EDGE, LANES), F32),
            pltpu.VMEM((2, crows + 2 * HALO, LANES), F32),
            pltpu.VMEM((levels, len(PAIRS), rows, cols), F32),
            pltpu.VMEM((len(PAIRS), rows, cols), F32),
            pltpu.VMEM((2, levels, len(ACROSS), EDGE, cols), F32),
            pltpu.VMEM((5, crows + 2 * HALO, ccols + LANES), F32),
            pltpu.VMEM((levels, cols // LANES, rows + 2 * EDGE, LANES), F32),
            pltpu.VMEM((levels, 3, cols // LANES, rows, LANES), F32),
            pltpu.VMEM((levels, len(ROWS), cols // LANES, rows + 2 * EDGE, LANES), F32),
            pltpu.VMEM((levels, 3, cols // LANES, rows, LANES), F32),
            pltpu.VMEM((2, 3, rows + 2 * EDGE, LANES), F32),
            pltpu.VMEM((COPIES + 1, LANES, LANES), BF16),
            pltpu.VMEM((2, LANES, levels * LANES), BF16),
            pltpu.VMEM((levels, rows, cols), F32),
            pltpu.VMEM((levels, rows, cols), F32),
            pltpu.VMEM((8, LANES), F32),
            pltpu.VMEM((group, 8, LANES), F32),
            pltpu.SemaphoreType.DMA((4 + cols // LANES + 2 * levels * REACH * groups,)),
            pltpu.SemaphoreType.DMA((n_moves,)),
            pltpu.SemaphoreType.DMA((n_moves,)),
            pltpu.SemaphoreType.DMA((group,)),
            pltpu.SemaphoreType.DMA((group,)),
        ],
        compiler_params=pltpu.CompilerParams(
            collective_id=0, has_side_effects=True, vmem_limit_bytes=62 << 20
        ),
    )(perturbations, coefficients, coarse_coefficients, residual, direction)
    new_iterate = iterate + step_length * direction
    new_residual = residual - step_length * q
    new_direction = new_residual + growth * direction
    return (new_iterate, new_residual, new_direction)


def solution(mesh):
    cell = P(None, "gx", "gy")
    return jax.shard_map(
        functools.partial(local, mesh.shape["gx"], mesh.shape["gy"]),
        mesh=mesh,
        in_specs=(P("ma", None, "gx", "gy"), cell, cell, cell, cell, cell),
        out_specs=(cell, cell, cell),
        check_vma=False,
    )
```

```python
import functools

import jax
import jax.numpy as jnp
from jax import lax
from jax.experimental import pallas as pl
from jax.experimental.pallas import tpu as pltpu
from jax.sharding import PartitionSpec as P

MEMBERS = 30
PASSES = 3
RATIO = 4
HALO = 4
LANES = 128
EDGE = 8
REACH = 3
PAIRS = (
    (0, 0), (0, 1), (0, 2), (0, 3), (1, 0), (2, 0), (3, 0), (1, 1), (1, 2), (2, 1),
    (-1, 1), (-1, 2), (-2, 1),
)
ACROSS = tuple((i, k) for i in (1, 2, 3) for k in range(i - 3, 4 - i))
ROWS = (-2, -1, 1, 2, 3)
MATRICES = tuple((0, True, k) for k in (1, 2)) + tuple((0, False, k) for k in (1, 2, 3))
MATRICES += tuple((1, True, k) for k in (1, 2, 3)) + tuple((1, False, k) for k in (1, 2))
COPIES = len(MATRICES)
MESH = pl.DeviceIdType.MESH
F32 = jnp.float32
BF16 = jnp.bfloat16


def shift_up(u, axis):
    return pltpu.roll(u, u.shape[axis] - 1, axis)


def shift_down(u, axis):
    return pltpu.roll(u, 1, axis)


def split_dot(a, b):
    high = a.astype(BF16)
    low = (a - high.astype(F32)).astype(BF16)
    return jnp.dot(high, b, preferred_element_type=F32) + jnp.dot(
        low, b, preferred_element_type=F32
    )


def stencil_weights(cx, cy, rows, cols, has_prev, has_next, has_left, has_right):
    ext_rows, ext_cols = cx.shape
    row = lax.broadcasted_iota(jnp.int32, (ext_rows, ext_cols), 0)
    col = lax.broadcasted_iota(jnp.int32, (ext_rows, ext_cols), 1)
    outside = (
        ((row >= rows) & (row < rows + HALO) & (has_next == 0))
        | ((row >= rows + HALO) & (has_prev == 0))
        | ((col >= cols) & (col < cols + LANES // 2) & (has_right == 0))
        | ((col >= cols + LANES // 2) & (has_left == 0))
    )
    xp = 0.5 * (cx + shift_up(cx, 0))
    xm = shift_down(xp, 0)
    yp = 0.5 * (cy + shift_up(cy, 1))
    ym = shift_down(yp, 1)
    centre = 1.0 - xp - xm - yp - ym
    return [jnp.where(outside, 0.0, value) for value in (centre, xp, xm, yp, ym)]


def shifted(u, dx, dy):
    if dx:
        u = pltpu.roll(u, -dx % u.shape[0], 0)
    if dy:
        u = pltpu.roll(u, -dy % u.shape[1], 1)
    return u


def composite(cx, cy, inside):
    s = shifted
    half_x = 0.5 * (cx + s(cx, 1, 0))
    half_y = 0.5 * (cy + s(cy, 0, 1))
    d = inside * (1.0 - half_x - s(half_x, -1, 0) - half_y - s(half_y, 0, -1))
    x = inside * s(inside, 1, 0) * half_x
    y = inside * s(inside, 0, 1) * half_y
    x2, y2 = x * x, y * y
    q = x2 + s(x2, -1, 0) + y2 + s(y2, 0, -1)
    dx, dy, dm = s(d, 1, 0), s(d, 0, 1), s(d, 0, -1)
    dxx, dyy, dxy, dxm = s(d, 2, 0), s(d, 0, 2), s(dy, 1, 0), s(dm, 1, 0)
    xx1, xy1, xm1 = s(x, 1, 0), s(x, 0, 1), s(x, 0, -1)
    yx1, yy1, ym = s(y, 1, 0), s(y, 0, 1), s(y, 0, -1)
    ymx = s(ym, 1, 0)
    xx, yy, xy, yx = x * xx1, y * yy1, x * yx1, y * xy1
    xym, ymx_then, ymym = x * ymx, ym * xm1, s(yy, 0, -2)
    u = {}
    u[0, 0] = d * (d * d + 2.0 * q) + x2 * dx + s(x2 * d, -1, 0) + y2 * dy + s(y2 * d, 0, -1)
    u[1, 0] = x * (d * d + d * dx + dx * dx + q + s(q, 1, 0) - x2) + yx * yx1 + ymx_then * ymx
    u[0, 1] = y * (d * d + d * dy + dy * dy + q + s(q, 0, 1) - y2) + xy * xy1 + s(x * yx, -1, 0)
    u[2, 0] = xx * (d + dx + dxx)
    u[0, 2] = yy * (d + dy + dyy)
    u[3, 0] = xx * s(x, 2, 0)
    u[0, 3] = yy * s(y, 0, 2)
    u[1, 1] = xy * (d + dx + dxy) + yx * (d + dy + dxy)
    u[1, -1] = xym * (d + dx + dxm) + ymx_then * (d + dm + dxm)
    u[2, 1] = xx * s(y, 2, 0) + x * s(yx, 1, 0) + y * s(xx, 0, 1)
    u[2, -1] = xx * s(ymx, 1, 0) + x * s(ymx_then, 1, 0) + ym * s(xx, 0, -1)
    u[1, 2] = x * s(yy, 1, 0) + y * s(xy, 0, 1) + yy * s(x, 0, 2)
    u[1, -2] = x * s(ymym, 1, 0) + ym * s(xym, 0, -1) + ymym * s(x, 0, -2)
    return u


def kernel(
    sizes,
    p_hbm, coef_hbm, ccoef_hbm, r_hbm, d_hbm,
    q_ref, step_ref, growth_ref,
    pv, coef_ref, ccoef_ref, r_ref, d_ref,
    wct, wch, line, lanes_out, packs, packs_y, packs_d, strips,
    rx_next, rx_prev, rc_next, rc_prev, ry, rd,
    cb, hv, hyc, sums_ref, inner, weights, coarse_weights, dv, dk, ev, fv, mv, copies, totals,
    acc, acc_other, part, slots,
    load_sem, send_sem, recv_sem, group_send, group_recv,
):
    n_x, n_y = sizes
    levels, rows, cols = d_ref.shape
    half, tiles = pv.shape[0], cols // LANES
    crows, ccols = ccoef_ref.shape[1], ccoef_ref.shape[2]
    gx, gy, ma = lax.axis_index("gx"), lax.axis_index("gy"), lax.axis_index("ma")
    me = gx * n_y + gy
    group = n_x * n_y
    has = {
        (-1, 0): gx > 0, (1, 0): gx < n_x - 1, (0, -1): gy > 0, (0, 1): gy < n_y - 1,
    }
    for dx in (-1, 1):
        for dy in (-1, 1):
            has[(dx, dy)] = has[(dx, 0)] & has[(0, dy)]

    def turned(at, count):
        return [at] + [
            jnp.where(at + k >= count, at + k - count, at + k) for k in range(1, count)
        ]

    if group <= 16:
        peers = [(x, y) for x in turned(gx, n_x) for y in turned(gy, n_y)][1:]

    def each_peer(action):
        if group <= 16:
            for x, y in peers:
                action(x, y)
            return

        def body(step, carry):
            k = lax.rem(me + step, group)
            action(k // n_y, k % n_y)
            return carry

        lax.fori_loop(1, group, body, 0)

    def lanes_of(j):
        return slice(j * LANES, (j + 1) * LANES)

    own = pl.ds(EDGE, rows)
    fields = half * levels
    bands = wct.shape[1]
    spans = [(g, pl.ds(8 * g, min(8, half - 8 * g))) for g in range(cb.shape[3])]
    loads = []

    def load(src, dst):
        loads.append(pltpu.make_async_copy(src, dst, load_sem.at[len(loads)]))
        loads[-1].start()

    load(d_hbm, d_ref)
    for j in range(tiles):
        load(p_hbm.at[:, :, :, pl.ds(j * LANES, LANES)], pv.at[:, :, j, own])
    load(coef_hbm, coef_ref)
    load(ccoef_hbm, ccoef_ref)
    load(r_hbm, r_ref)
    early = len(loads)

    barrier = pltpu.get_barrier_semaphore()
    pl.semaphore_signal(barrier, inc=1, device_id={"ma": 1 - ma}, device_id_type=MESH)
    each_peer(
        lambda x, y: pl.semaphore_signal(
            barrier, inc=1, device_id={"gx": x, "gy": y}, device_id_type=MESH
        )
    )
    for side in (0, 1):
        for level in range(levels):
            for e in range(REACH):
                x = rows - 1 - e if side else e
                for g, span in spans:
                    load(p_hbm.at[span, level, x], cb.at[side, level, REACH + e, g, pl.ds(0, span.size)])

    def zero_if(absent, ref):
        @pl.when(absent)
        def _():
            ref[...] = jnp.zeros_like(ref)

    zero_if(gx == 0, rx_prev)
    zero_if(gx == 0, rc_prev)
    zero_if(gx == n_x - 1, rx_next)
    zero_if(gx == n_x - 1, rc_next)
    rest = -half % 8
    for g, span in spans:
        zero_if(gx == 0, cb.at[0, :, pl.ds(0, REACH), g, pl.ds(0, span.size)])
        zero_if(gx == n_x - 1, cb.at[1, :, pl.ds(0, REACH), g, pl.ds(0, span.size)])
    if rest:
        cb[:, :, :, cb.shape[3] - 1, 8 - rest :] = jnp.zeros((2, levels, 2 * REACH, rest, cols), F32)
    pv[:, :, :, :EDGE] = jnp.zeros((half, levels, tiles, EDGE, LANES), F32)
    pv[:, :, :, EDGE + rows :] = jnp.zeros((half, levels, tiles, EDGE, LANES), F32)
    zero_if(gx == 0, wct.at[pl.ds(HALO - REACH, REACH)])
    zero_if(gx == n_x - 1, wct.at[pl.ds(HALO + crows, REACH)])
    for x in (0, 2 * HALO + crows - 1):
        wct[x] = jnp.zeros((bands, 8, LANES), F32)
    for f in range(fields, 8 * bands):
        line[f * rows : (f + 1) * rows] = jnp.zeros((rows, ccols), F32)
    for side in (0, 1):
        dy = 2 * side - 1
        zero_if(jnp.logical_not(has[(0, dy)]), ry.at[side])
        zero_if(jnp.logical_not(has[(0, dy)]), packs_y.at[side])
        for way in (0, 1):
            zero_if(jnp.logical_not(has[(2 * way - 1, dy)]), rd.at[side, way])
            zero_if(jnp.logical_not(has[(2 * way - 1, dy)]), packs_d.at[side, way])

    moves = []

    def move(src, dst, dx, dy):
        slot = len(moves)
        target = {
            "gx": jnp.clip(gx + dx, 0, n_x - 1) if dx else gx,
            "gy": jnp.clip(gy + dy, 0, n_y - 1) if dy else gy,
        }
        copy = pltpu.make_async_remote_copy(
            src_ref=src, dst_ref=dst, send_sem=send_sem.at[slot], recv_sem=recv_sem.at[slot],
            device_id=target, device_id_type=MESH,
        )
        moves.append((copy, has[(dx, dy)], has[(-dx, -dy)]))

        @pl.when(has[(dx, dy)])
        def _():
            copy.start()

        return slot

    def arrive(slot):
        @pl.when(moves[slot][2])
        def _():
            moves[slot][0].wait_recv()

    def move_rows(level):
        slots_of = []
        for h in range(REACH):
            for g, span in spans:
                for side, x in ((1, h), (0, rows - 1 - h)):
                    dst = cb.at[side, level, h, g, pl.ds(0, span.size)]
                    slots_of.append(move(p_hbm.at[span, level, x], dst, 1 - 2 * side, 0))
        return slots_of

    for copy in loads[:early]:
        copy.wait()
    flane = lax.broadcasted_iota(jnp.int32, (rows, LANES), 1)
    blane = lax.broadcasted_iota(jnp.int32, (8, LANES), 1)
    lane = blane
    clane = lax.broadcasted_iota(jnp.int32, (crows, LANES), 1)
    fl = fr = jnp.zeros((rows, LANES), F32)
    cl = cr = jnp.zeros((crows, LANES), F32)
    for f in (0, 1):
        at = PASSES * f
        field = ccoef_ref[f]
        cl = jnp.where(
            clane >= at, pltpu.roll(field[:, :LANES], at, 1) if at else field[:, :LANES], cl
        )
        cr = jnp.where(clane >= at, pltpu.roll(field[:, ccols - LANES :], at + PASSES, 1), cr)
    for f in range(fields + 2 + levels):
        at = PASSES * f
        if f < fields:
            first = pv[f // levels, f % levels, 0, EDGE : EDGE + rows]
            last = pv[f // levels, f % levels, tiles - 1, EDGE : EDGE + rows]
        elif f < fields + 2:
            first = coef_ref[f - fields, :, :LANES]
            last = coef_ref[f - fields, :, cols - LANES :]
        else:
            first = d_ref[f - fields - 2, :, :LANES]
            last = d_ref[f - fields - 2, :, cols - LANES :]
        fl = jnp.where(flane >= at, pltpu.roll(first, at, 1) if at else first, fl)
        fr = jnp.where(flane >= at, pltpu.roll(last, at + PASSES, 1), fr)
    for side, (fine, small) in enumerate(((fl, cl), (fr, cr))):
        strips[side, 0:crows] = small
        strips[side, crows : crows + rows] = fine
        strips[side, crows + rows :] = small
    for level in range(levels):
        for j in range(tiles):
            here = d_ref[level, :, lanes_of(j)]
            there = d_ref[level, :, lanes_of((j + 1) % tiles)]
            dv[level, j, :EDGE] = jnp.zeros((EDGE, LANES), F32)
            dv[level, j, EDGE : EDGE + rows] = here
            dv[level, j, EDGE + rows :] = jnp.zeros((EDGE, LANES), F32)
            for k in (1, 2, 3):
                dk[level, k - 1, j] = jnp.where(
                    flane < LANES - k,
                    pltpu.roll(here, LANES - k, 1),
                    pltpu.roll(there, LANES - k, 1),
                )
            for t in range(len(ROWS)):
                ev[level, t, j, :EDGE] = jnp.zeros((EDGE, LANES), F32)
                ev[level, t, j, EDGE + rows :] = jnp.zeros((EDGE, LANES), F32)
    lin = lax.broadcasted_iota(jnp.int32, (LANES, LANES), 0)
    lout = lax.broadcasted_iota(jnp.int32, (LANES, LANES), 1)
    step = lax.rem(lout, PASSES)
    inside = lout < PASSES * fields
    for n, (side, ahead, k) in enumerate(MATRICES):
        if side:
            source = step + (LANES - PASSES if ahead else k - PASSES)
            hit = (lin == source) & (step >= PASSES - k) & inside
        else:
            source = step if ahead else step + (LANES - k)
            hit = (lin == source) & (step < k) & inside
        copies[n] = jnp.where(hit, 1.0, 0.0).astype(BF16)
    period = PASSES * levels
    hit = (lin - PASSES * (fields + 2) == lax.rem(lout, period)) & inside
    copies[COPIES] = jnp.where(hit, 1.0, 0.0).astype(BF16)
    for level in range(levels):
        source = lax.rem(lin, period) - PASSES * level
        for side in (0, 1):
            place = lout - (LANES - PASSES) * side
            hit = (source == place) & (place >= 0) & (place < PASSES) & (lin < PASSES * fields)
            totals[side, :, lanes_of(level)] = jnp.where(hit, 1.0, 0.0).astype(BF16)

    pl.semaphore_wait(barrier, group)
    e_moves = []
    for k, (src, count) in enumerate(((coef_hbm, 2), (d_hbm, levels))):
        span = pl.ds(2 * k, count)
        e_moves.append(move(src.at[:, pl.ds(0, HALO)], rx_next.at[span], -1, 0))
        e_moves.append(move(src.at[:, pl.ds(rows - HALO, HALO)], rx_prev.at[span], 1, 0))
    e_moves.append(move(ccoef_hbm.at[:, pl.ds(0, HALO)], rc_next, -1, 0))
    e_moves.append(move(ccoef_hbm.at[:, pl.ds(crows - HALO, HALO)], rc_prev, 1, 0))
    y_moves = []
    for side in (0, 1):
        dy = 2 * side - 1
        other = 1 - side
        y_moves.append(move(strips.at[side, pl.ds(0, crows + rows)], ry.at[other], 0, dy))
        y_moves.append(move(strips.at[side, pl.ds(0, crows + 8)], rd.at[other, 1], -1, dy))
        y_moves.append(
            move(strips.at[side, pl.ds(crows + rows - 8, crows + 8)], rd.at[other, 0], 1, dy)
        )
    row_moves = [move_rows(0)]

    pick = lax.broadcasted_iota(jnp.int32, (cols, ccols), 0) // RATIO
    gather = jnp.where(
        pick == lax.broadcasted_iota(jnp.int32, (cols, ccols), 1), 1.0 / RATIO**2, 0.0
    ).astype(BF16)
    batch = next(k for k in (5, 3, 2, 1) if half % k == 0)

    def restrict(n, carry):
        tall = batch * levels * rows
        values = jnp.concatenate(
            [
                (
                    pv[pl.ds(n * batch, batch), :, j, EDGE : EDGE + rows]
                    * d_ref[:, :, lanes_of(j)][None]
                ).reshape(tall, LANES)
                for j in range(tiles)
            ],
            axis=1,
        )
        line[pl.ds(pl.multiple_of(n * tall, 8), tall)] = split_dot(values, gather)
        return carry

    lax.fori_loop(0, half // batch, restrict, 0)
    for x in range(crows):
        for g in range(bands):
            value = None
            for k in range(RATIO):
                term = line[pl.ds(g * 8 * rows + RATIO * x + k, 8, stride=rows), :]
                value = term if k == 0 else value + term
            wct[HALO + x, g] = value

    for g in range(bands):
        for side in (0, 1):
            value = jnp.zeros((8, LANES), F32)
            for x in range(crows):
                at = PASSES * x
                turn = at + PASSES * side
                field = wct[HALO + x, g]
                value = jnp.where(blane >= at, pltpu.roll(field, turn, 1) if turn else field, value)
            packs[side, g] = value
    c_moves = []
    for side in (0, 1):
        dy = 2 * side - 1
        c_moves.append(move(packs.at[side], packs_y.at[1 - side], 0, dy))
        c_moves.append(move(packs.at[side], packs_d.at[1 - side, 1], -1, dy))
        c_moves.append(move(packs.at[side], packs_d.at[1 - side, 0], 1, dy))
    c_moves.append(
        move(wct.at[pl.ds(HALO, REACH)], wct.at[pl.ds(HALO + crows, REACH)], -1, 0)
    )
    c_moves.append(
        move(wct.at[pl.ds(HALO + crows - REACH, REACH)], wct.at[pl.ds(HALO - REACH, REACH)], 1, 0)
    )
    for level in range(1, levels):
        row_moves.append(move_rows(level))

    def products(n, carry):
        level = n // (rows // 8)
        at = pl.multiple_of(n % (rows // 8) * 8, 8)
        for j in range(0, tiles, 2):
            total = [[None] * len(PAIRS), [None] * len(PAIRS)]
            for m in range(half):
                here = [pv[m, level, (j + g) % tiles, pl.ds(at + EDGE, 8)] for g in range(3)]
                turned = [[pltpu.roll(v, LANES - k, 1) for v in here] for k in (1, 2, 3)]
                for g in range(2):
                    below = {
                        i: pv[m, level, j + g, pl.ds(at + EDGE + i, 8)] if i else here[g]
                        for i in range(-2, 4)
                    }
                    right = [here[g]] + [
                        jnp.where(lane < LANES - k, turned[k - 1][g], turned[k - 1][g + 1])
                        for k in (1, 2, 3)
                    ]
                    for t, (i, k) in enumerate(PAIRS):
                        v = below[i] * right[k]
                        total[g][t] = v if m == 0 else total[g][t] + v
            for g in range(2):
                for t in range(len(PAIRS)):
                    sums_ref[level, t, pl.ds(at, 8), lanes_of(j + g)] = total[g][t]
        return carry

    lax.fori_loop(0, levels * (rows // 8), products, 0)

    for slot in e_moves:
        arrive(slot)
    for slot in y_moves:
        arrive(slot)

    near = lax.broadcasted_iota(jnp.int32, (8, LANES), 0) < HALO
    for side in (0, 1):
        hyc[side, 0:crows] = ry[side, 0:crows]
        hyc[side, crows : crows + 8] = jnp.where(
            near, rd[side, 1, 0:8], rd[side, 0, crows : crows + 8]
        )
        hv[side, 0:EDGE] = rd[side, 0, 0:8]
        hv[side, EDGE : EDGE + rows] = ry[side, crows : crows + rows]
        hv[side, EDGE + rows :] = rd[side, 1, crows : crows + 8]

    def columns(ref, index, height):
        lane = lax.broadcasted_iota(jnp.int32, (height, LANES), 1)
        at = PASSES * index
        right = pltpu.roll(ref[1], LANES - at, 1)
        left = pltpu.roll(ref[0], LANES - PASSES - at, 1)
        return jnp.where(
            lane < PASSES, right, jnp.where(lane >= LANES - PASSES, left, 0.0)
        )

    def coarse_field(f):
        height = crows + 2 * HALO
        tall = jnp.concatenate(
            [ccoef_ref[f], jnp.concatenate([rc_next[f], rc_prev[f]], axis=0)], axis=0
        )
        return jnp.concatenate([tall, columns(hyc, f, height)], axis=1)

    ext_rows, ext_cols = rows + 2 * EDGE, cols + LANES

    def wide(main, index):
        pad = jnp.zeros((EDGE - HALO, cols), F32)
        tall = jnp.concatenate(
            [
                jnp.concatenate([pad, rx_prev[index]], axis=0),
                main,
                jnp.concatenate([rx_next[index], pad], axis=0),
            ],
            axis=0,
        )
        return jnp.concatenate([tall, columns(hv, fields + index, ext_rows)], axis=1)

    ends = [
        value.astype(jnp.int32)
        for value in (has[(-1, 0)], has[(1, 0)], has[(0, -1)], has[(0, 1)])
    ]
    row = lax.broadcasted_iota(jnp.int32, (ext_rows, ext_cols), 0) - EDGE
    col = lax.broadcasted_iota(jnp.int32, (ext_rows, ext_cols), 1)
    outside = (
        ((row < 0) & (ends[0] == 0))
        | ((row >= rows) & (ends[1] == 0))
        | ((col >= cols + LANES // 2) & (ends[2] == 0))
        | ((col >= cols) & (col < cols + LANES // 2) & (ends[3] == 0))
    )
    u = composite(wide(coef_ref[0], 0), wide(coef_ref[1], 1), jnp.where(outside, 0.0, 1.0))

    row = lax.broadcasted_iota(jnp.int32, (rows, cols), 0)
    col = lax.broadcasted_iota(jnp.int32, (rows, cols), 1)
    for t, (i, k) in enumerate(PAIRS):
        if i >= 0:
            value = shifted(u[i, -k], 0, k) if i and k else u[i, k]
            valid = (row < rows - i) & (col < cols - k)
        else:
            value = shifted(u[-i, k], i, 0)
            valid = (row >= -i) & (col < cols - k)
        inner[t] = jnp.where(valid, value[EDGE : EDGE + rows, :cols], 0.0)

    ecol = lax.broadcasted_iota(jnp.int32, (EDGE, cols), 1)
    d_wide = [wide(d_ref[level], 2 + level) for level in range(levels)]
    for side in (0, 1):
        span = slice(rows, rows + 2 * EDGE) if side else slice(0, 2 * EDGE)
        take = slice(0, EDGE) if side else slice(EDGE, 2 * EDGE)
        for n, (i, k) in enumerate(ACROSS):
            move_x = i if side else -i
            if side:
                value = u[i, k][span]
            else:
                value = shifted(u[i, -k][span], move_x, k)
            valid = (ecol + k >= 0) & (ecol + k < cols)
            value = jnp.where(valid, value[take, :cols], 0.0)
            for level in range(levels):
                near_d = shifted(d_wide[level][span], move_x, k)[take, :cols]
                weights[side, level, n] = value * near_d

    edge_sums = []
    for side in (0, 1):
        halo_d = split_dot(hv[side], copies[COPIES])
        weighted = hv[side] * halo_d
        for k in (1, 2, 3):
            away = PASSES - k
            turn = away if side else -away % LANES
            mv[side, k - 1] = pltpu.roll(weighted, turn, 1) if away else weighted
        value = jnp.zeros((rows, LANES), F32)
        for n in range(COPIES):
            which, ahead, k = MATRICES[n]
            if which != side:
                continue
            stack, steps = [], []
            for i in range(k - 3, 4 - k):
                if side and ahead and i >= 0:
                    w = u[i, k][:, cols - LANES : cols]
                elif side and not ahead and i < 0:
                    w = shifted(u[-i, -k][:, cols:], i, 0)
                elif not side and ahead and i > 0:
                    w = u[i, -k][:, :LANES]
                elif not side and not ahead and i <= 0:
                    w = shifted(u[-i, k][:, cols:], i, 0)
                else:
                    continue
                stack.append(w[EDGE : EDGE + rows])
                steps.append(i)
            w = split_dot(jnp.concatenate(stack, axis=0), copies[n])
            for t, i in enumerate(steps):
                value = value + w[t * rows : (t + 1) * rows] * mv[side, k - 1, EDGE + i : EDGE + i + rows]
        value = value * strips[side, crows : crows + rows]
        edge_sums.append(split_dot(value, totals[side]))

    def combine(n, carry):
        level = n // (rows // 8)
        at = pl.multiple_of(n % (rows // 8) * 8, 8)
        for j in range(tiles):
            d_right = [dv[level, j, pl.ds(at + EDGE, 8)]] + [
                dk[level, k - 1, j, pl.ds(at, 8)] for k in (1, 2, 3)
            ]
            d_below = {
                i: dv[level, j, pl.ds(at + EDGE + i, 8)] if i else d_right[0] for i in range(-2, 4)
            }
            up, across = {}, {}
            for t, (i, k) in enumerate(PAIRS):
                value = (
                    inner[t, pl.ds(at, 8), lanes_of(j)]
                    * sums_ref[level, t, pl.ds(at, 8), lanes_of(j)]
                )
                term = value * d_right[k]
                up[i] = up[i] + term if i in up else term
                if i or k:
                    term = value * d_below[i]
                    across[k] = across[k] + term if k in across else term
            acc[level, pl.ds(at, 8), lanes_of(j)] = up[0] + across[0]
            for t, i in enumerate(ROWS):
                ev[level, t, j, pl.ds(at + EDGE, 8)] = up[i]
            for k in (1, 2, 3):
                fv[level, k - 1, j, pl.ds(at, 8)] = across[k]
        return carry

    lax.fori_loop(0, levels * (rows // 8), combine, 0, unroll=2)

    def collect(n, carry):
        level = n // (rows // 8)
        at = pl.multiple_of(n % (rows // 8) * 8, 8)
        turned = [
            [pltpu.roll(fv[level, k - 1, j, pl.ds(at, 8)], k, 1) for j in range(tiles)]
            for k in (1, 2, 3)
        ]
        for j in range(tiles):
            total = acc[level, pl.ds(at, 8), lanes_of(j)]
            for t, i in enumerate(ROWS):
                total = total + ev[level, t, j, pl.ds(at + EDGE - i, 8)]
            for k in (1, 2, 3):
                total = total + jnp.where(lane >= k, turned[k - 1][j], turned[k - 1][j - 1])
            acc[level, pl.ds(at, 8), lanes_of(j)] = total
        return carry

    lax.fori_loop(0, levels * (rows // 8), collect, 0, unroll=2)
    for level in range(levels):
        at = slice(level * LANES, (level + 1) * LANES)
        acc[level, :, :LANES] += edge_sums[0][:, at]
        acc[level, :, cols - LANES :] += edge_sums[1][:, at]

    for slot in c_moves:
        arrive(slot)
    for k, value in enumerate(
        stencil_weights(coarse_field(0), coarse_field(1), crows, ccols, *ends)
    ):
        coarse_weights[k] = value
    for x in range(-REACH, crows + REACH):
        for g in range(bands):
            way = 0 if x < 0 else 1
            inner_row = 0 <= x < crows
            left = packs_y[0, g] if inner_row else packs_d[0, way, g]
            right = packs_y[1, g] if inner_row else packs_d[1, way, g]
            at = PASSES * (x % crows)
            if at:
                right = pltpu.roll(right, LANES - at, 1)
            left = pltpu.roll(left, LANES - PASSES - at, 1)
            wch[0, HALO + x, g] = jnp.where(
                blane < PASSES, right, jnp.where(blane >= LANES - PASSES, left, 0.0)
            )
    for step in range(PASSES):
        low = HALO - REACH + 1 + step
        source = [wct, wch.at[0]] if step == 0 else [wch.at[2 * step - 1], wch.at[2 * step]]
        last = step == PASSES - 1

        def coarse_row(x, carry):
            w = [
                [coarse_weights[k, pl.ds((x + crows + HALO) % (crows + 2 * HALO), 1),
                                lanes_of(q)] for k in range(5)]
                for q in range(1 if last else 2)
            ]
            for g in range(bands):
                here = [source[q][x, g] for q in (0, 1)]
                ahead = [pltpu.roll(v, LANES - 1, 1) for v in here]
                back = [pltpu.roll(v, 1, 1) for v in here]
                for q in range(1 if last else 2):
                    value = (
                        w[q][0] * here[q]
                        + w[q][1] * source[q][x + 1, g]
                        + w[q][2] * source[q][x - 1, g]
                        + w[q][3] * jnp.where(blane < LANES - 1, ahead[q], ahead[1 - q])
                        + w[q][4] * jnp.where(blane >= 1, back[q], back[1 - q])
                    )
                    if last:
                        at = pl.multiple_of(((x - HALO) * bands + g) * 8, 8)
                        line[pl.ds(at, 8)] = value
                    else:
                        wch[2 * step + 1 + q, x, g] = value
            return carry

        for x in range(low, crows + 2 * HALO - low):
            coarse_row(x, 0)
    spread = jnp.where(
        lax.broadcasted_iota(jnp.int32, (ccols, cols), 1) // RATIO
        == lax.broadcasted_iota(jnp.int32, (ccols, cols), 0),
        1.0, 0.0,
    ).astype(BF16)
    wide_rows = split_dot(line[pl.ds(0, crows * bands * 8)], spread)
    for j in range(tiles):
        lanes_out[j] = wide_rows[:, lanes_of(j)]

    upper = lax.broadcasted_iota(jnp.int32, (8, LANES), 0) < RATIO

    def add_coarse(n, carry):
        level, t = n // (rows // 8), n % (rows // 8)
        at = pl.multiple_of(t * 8, 8)
        for j in range(tiles):
            total = None
            for m in range(half):
                base = 2 * t * (8 * bands) + m * levels + level
                a = jnp.broadcast_to(lanes_out[j, pl.ds(base, 1)], (8, LANES))
                b = jnp.broadcast_to(lanes_out[j, pl.ds(base + 8 * bands, 1)], (8, LANES))
                v = pv[m, level, j, pl.ds(at + EDGE, 8)] * jnp.where(upper, a, b)
                total = v if m == 0 else total + v
            acc[level, pl.ds(at, 8), lanes_of(j)] += total
        return carry

    lax.fori_loop(0, levels * (rows // 8), add_coarse, 0)

    for copy in loads[early:]:
        copy.wait()
    for level in range(levels):
        for slot in row_moves[level]:
            arrive(slot)
        for side in (0, 1):
            for j in range(tiles):
                total = [None] * REACH
                for g in range(cb.shape[3]):
                    def tile(r, at):
                        return cb[side, level, r, g, :, lanes_of(at % tiles)]

                    halo = {}
                    for h in range(REACH):
                        halo[h, 0] = tile(h, j)
                        for k in range(1, REACH - h):
                            halo[h, k] = jnp.where(
                                lane < LANES - k,
                                pltpu.roll(tile(h, j), LANES - k, 1),
                                pltpu.roll(tile(h, j + 1), LANES - k, 1),
                            )
                            halo[h, -k] = jnp.where(
                                lane >= k,
                                pltpu.roll(tile(h, j), k, 1),
                                pltpu.roll(tile(h, j - 1), k, 1),
                            )
                    for e in range(REACH):
                        x = EDGE - 1 - e if side else e
                        value = None
                        for h in range(REACH - e):
                            i = e + h + 1
                            for k in range(i - 3, 4 - i):
                                w = weights[side, level, ACROSS.index((i, k)), x : x + 1, lanes_of(j)]
                                term = w * halo[h, k]
                                value = term if value is None else value + term
                        value = value * tile(REACH + e, j)
                        total[e] = value if g == 0 else total[e] + value
                for e in range(REACH):
                    x = rows - 1 - e if side else e
                    acc[level, x : x + 1, lanes_of(j)] += jnp.sum(total[e], axis=0, keepdims=True)

    swap = pltpu.make_async_remote_copy(
        src_ref=acc, dst_ref=acc_other, send_sem=send_sem.at[len(moves)],
        recv_sem=recv_sem.at[len(moves)], device_id={"ma": 1 - ma}, device_id_type=MESH,
    )
    swap.start()
    swap.wait_recv()
    d, r = d_ref[...], r_ref[...]
    q = d + (acc[...] + acc_other[...]) / (MEMBERS - 1)
    q_ref[...] = q

    def total_row(value):
        flat = value.reshape(levels * rows // 8, 8, cols)
        tile = jnp.sum(flat, axis=0)
        narrow = tile[:, :LANES]
        for k in range(1, cols // LANES):
            narrow = narrow + tile[:, k * LANES : (k + 1) * LANES]
        return jnp.sum(narrow, axis=0, keepdims=True)

    row = lax.broadcasted_iota(jnp.int32, (8, LANES), 0)
    packed = jnp.zeros((8, LANES), F32)
    for k, value in enumerate((r * r, d * q, r * q, q * q)):
        packed = jnp.where(row == k, total_row(value), packed)
    part[...] = packed
    slots[me] = packed

    def to_peer(x, y):
        k = x * n_y + y
        return pltpu.make_async_remote_copy(
            src_ref=part, dst_ref=slots.at[me], send_sem=group_send.at[k],
            recv_sem=group_recv.at[me],
            device_id={"gx": x, "gy": y}, device_id_type=MESH,
        )

    def from_peer(x, y):
        k = x * n_y + y
        return pltpu.make_async_remote_copy(
            src_ref=part, dst_ref=slots.at[k], send_sem=group_send.at[k],
            recv_sem=group_recv.at[k],
            device_id={"gx": x, "gy": y}, device_id_type=MESH,
        )

    each_peer(lambda x, y: to_peer(x, y).start())
    swap.wait_send()
    for copy, sends, _ in moves:
        @pl.when(sends)
        def _():
            copy.wait_send()
    each_peer(lambda x, y: from_peer(x, y).wait_recv())
    sums = jnp.sum(jnp.sum(slots[...], axis=0), axis=1, keepdims=True)
    norm_old, curvature, cross, image = (sums[k : k + 1] for k in range(4))
    step_length = norm_old / curvature
    norm_new = norm_old + step_length * (step_length * image - 2.0 * cross)
    step_ref[...] = jnp.broadcast_to(step_length, (1, cols))
    growth_ref[...] = jnp.broadcast_to(norm_new / norm_old, (1, cols))
    each_peer(lambda x, y: to_peer(x, y).wait_send())


def local(n_x, n_y, perturbations, coefficients, coarse_coefficients, iterate, residual, direction):
    half, levels, rows, cols = perturbations.shape
    _, crows, ccols = coarse_coefficients.shape
    group = n_x * n_y
    groups = -(-half // 8)
    bands = -(-half * levels // 8)
    n_moves = 6 + 2 * REACH * levels * groups + 6 + 8 + 1
    vmem = pl.BlockSpec(memory_space=pltpu.VMEM)
    q, step_length, growth = pl.pallas_call(
        functools.partial(kernel, (n_x, n_y)),
        out_shape=(
            jax.ShapeDtypeStruct((levels, rows, cols), F32),
            jax.ShapeDtypeStruct((1, cols), F32),
            jax.ShapeDtypeStruct((1, cols), F32),
        ),
        in_specs=[pl.BlockSpec(memory_space=pltpu.HBM)] * 5,
        out_specs=(vmem, vmem, vmem),
        scratch_shapes=[
            pltpu.VMEM((half, levels, cols // LANES, rows + 2 * EDGE, LANES), F32),
            pltpu.VMEM((2, rows, cols), F32),
            pltpu.VMEM((2, crows, ccols), F32),
            pltpu.VMEM((levels, rows, cols), F32),
            pltpu.VMEM((levels, rows, cols), F32),
            pltpu.VMEM((crows + 2 * HALO, bands, 8, LANES), F32),
            pltpu.VMEM((2 * PASSES - 1, crows + 2 * HALO, bands, 8, LANES), F32),
            pltpu.VMEM((8 * bands * rows, ccols), F32),
            pltpu.VMEM((cols // LANES, 8 * bands * crows, LANES), F32),
            pltpu.VMEM((2, bands, 8, LANES), F32),
            pltpu.VMEM((2, bands, 8, LANES), F32),
            pltpu.VMEM((2, 2, bands, 8, LANES), F32),
            pltpu.VMEM((2, rows + 2 * crows, LANES), F32),
            pltpu.VMEM((2 + levels, HALO, cols), F32),
            pltpu.VMEM((2 + levels, HALO, cols), F32),
            pltpu.VMEM((2, HALO, ccols), F32),
            pltpu.VMEM((2, HALO, ccols), F32),
            pltpu.VMEM((2, rows + crows, LANES), F32),
            pltpu.VMEM((2, 2, crows + 8, LANES), F32),
            pltpu.VMEM((2, levels, 2 * REACH, groups, 8, cols), F32),
            pltpu.VMEM((2, rows + 2 * EDGE, LANES), F32),
            pltpu.VMEM((2, crows + 2 * HALO, LANES), F32),
            pltpu.VMEM((levels, len(PAIRS), rows, cols), F32),
            pltpu.VMEM((len(PAIRS), rows, cols), F32),
            pltpu.VMEM((2, levels, len(ACROSS), EDGE, cols), F32),
            pltpu.VMEM((5, crows + 2 * HALO, ccols + LANES), F32),
            pltpu.VMEM((levels, cols // LANES, rows + 2 * EDGE, LANES), F32),
            pltpu.VMEM((levels, 3, cols // LANES, rows, LANES), F32),
            pltpu.VMEM((levels, len(ROWS), cols // LANES, rows + 2 * EDGE, LANES), F32),
            pltpu.VMEM((levels, 3, cols // LANES, rows, LANES), F32),
            pltpu.VMEM((2, 3, rows + 2 * EDGE, LANES), F32),
            pltpu.VMEM((COPIES + 1, LANES, LANES), BF16),
            pltpu.VMEM((2, LANES, levels * LANES), BF16),
            pltpu.VMEM((levels, rows, cols), F32),
            pltpu.VMEM((levels, rows, cols), F32),
            pltpu.VMEM((8, LANES), F32),
            pltpu.VMEM((group, 8, LANES), F32),
            pltpu.SemaphoreType.DMA((4 + cols // LANES + 2 * levels * REACH * groups,)),
            pltpu.SemaphoreType.DMA((n_moves,)),
            pltpu.SemaphoreType.DMA((n_moves,)),
            pltpu.SemaphoreType.DMA((group,)),
            pltpu.SemaphoreType.DMA((group,)),
        ],
        compiler_params=pltpu.CompilerParams(
            collective_id=0, has_side_effects=True, vmem_limit_bytes=62 << 20
        ),
    )(perturbations, coefficients, coarse_coefficients, residual, direction)
    new_iterate = iterate + step_length * direction
    new_residual = residual - step_length * q
    new_direction = new_residual + growth * direction
    return (new_iterate, new_residual, new_direction)


def solution(mesh):
    cell = P(None, "gx", "gy")
    return jax.shard_map(
        functools.partial(local, mesh.shape["gx"], mesh.shape["gy"]),
        mesh=mesh,
        in_specs=(P("ma", None, "gx", "gy"), cell, cell, cell, cell, cell),
        out_specs=(cell, cell, cell),
        check_vma=False,
    )
```

```python
import functools

import jax
import jax.numpy as jnp
from jax import lax
from jax.experimental import pallas as pl
from jax.experimental.pallas import tpu as pltpu
from jax.sharding import PartitionSpec as P

MEMBERS = 30
PASSES = 3
RATIO = 4
HALO = 4
LANES = 128
EDGE = 8
REACH = 3
PAIRS = (
    (0, 0), (0, 1), (0, 2), (0, 3), (1, 0), (2, 0), (3, 0), (1, 1), (1, 2), (2, 1),
    (-1, 1), (-1, 2), (-2, 1),
)
ACROSS = tuple((i, k) for i in (1, 2, 3) for k in range(i - 3, 4 - i))
ROWS = (-2, -1, 1, 2, 3)
MATRICES = tuple((0, True, k) for k in (1, 2)) + tuple((0, False, k) for k in (1, 2, 3))
MATRICES += tuple((1, True, k) for k in (1, 2, 3)) + tuple((1, False, k) for k in (1, 2))
COPIES = len(MATRICES)
MESH = pl.DeviceIdType.MESH
F32 = jnp.float32
BF16 = jnp.bfloat16


def shift_up(u, axis):
    return pltpu.roll(u, u.shape[axis] - 1, axis)


def shift_down(u, axis):
    return pltpu.roll(u, 1, axis)


def split_dot(a, b):
    high = a.astype(BF16)
    low = (a - high.astype(F32)).astype(BF16)
    return jnp.dot(high, b, preferred_element_type=F32) + jnp.dot(
        low, b, preferred_element_type=F32
    )


def stencil_weights(cx, cy, rows, cols, has_prev, has_next, has_left, has_right):
    ext_rows, ext_cols = cx.shape
    row = lax.broadcasted_iota(jnp.int32, (ext_rows, ext_cols), 0)
    col = lax.broadcasted_iota(jnp.int32, (ext_rows, ext_cols), 1)
    outside = (
        ((row >= rows) & (row < rows + HALO) & (has_next == 0))
        | ((row >= rows + HALO) & (has_prev == 0))
        | ((col >= cols) & (col < cols + LANES // 2) & (has_right == 0))
        | ((col >= cols + LANES // 2) & (has_left == 0))
    )
    xp = 0.5 * (cx + shift_up(cx, 0))
    xm = shift_down(xp, 0)
    yp = 0.5 * (cy + shift_up(cy, 1))
    ym = shift_down(yp, 1)
    centre = 1.0 - xp - xm - yp - ym
    return [jnp.where(outside, 0.0, value) for value in (centre, xp, xm, yp, ym)]


def shifted(u, dx, dy):
    if dx:
        u = pltpu.roll(u, -dx % u.shape[0], 0)
    if dy:
        u = pltpu.roll(u, -dy % u.shape[1], 1)
    return u


def composite(cx, cy, inside):
    s = shifted
    half_x = 0.5 * (cx + s(cx, 1, 0))
    half_y = 0.5 * (cy + s(cy, 0, 1))
    d = inside * (1.0 - half_x - s(half_x, -1, 0) - half_y - s(half_y, 0, -1))
    x = inside * s(inside, 1, 0) * half_x
    y = inside * s(inside, 0, 1) * half_y
    x2, y2 = x * x, y * y
    q = x2 + s(x2, -1, 0) + y2 + s(y2, 0, -1)
    dx, dy, dm = s(d, 1, 0), s(d, 0, 1), s(d, 0, -1)
    dxx, dyy, dxy, dxm = s(d, 2, 0), s(d, 0, 2), s(dy, 1, 0), s(dm, 1, 0)
    xx1, xy1, xm1 = s(x, 1, 0), s(x, 0, 1), s(x, 0, -1)
    yx1, yy1, ym = s(y, 1, 0), s(y, 0, 1), s(y, 0, -1)
    ymx = s(ym, 1, 0)
    xx, yy, xy, yx = x * xx1, y * yy1, x * yx1, y * xy1
    xym, ymx_then, ymym = x * ymx, ym * xm1, s(yy, 0, -2)
    u = {}
    u[0, 0] = d * (d * d + 2.0 * q) + x2 * dx + s(x2 * d, -1, 0) + y2 * dy + s(y2 * d, 0, -1)
    u[1, 0] = x * (d * d + d * dx + dx * dx + q + s(q, 1, 0) - x2) + yx * yx1 + ymx_then * ymx
    u[0, 1] = y * (d * d + d * dy + dy * dy + q + s(q, 0, 1) - y2) + xy * xy1 + s(x * yx, -1, 0)
    u[2, 0] = xx * (d + dx + dxx)
    u[0, 2] = yy * (d + dy + dyy)
    u[3, 0] = xx * s(x, 2, 0)
    u[0, 3] = yy * s(y, 0, 2)
    u[1, 1] = xy * (d + dx + dxy) + yx * (d + dy + dxy)
    u[1, -1] = xym * (d + dx + dxm) + ymx_then * (d + dm + dxm)
    u[2, 1] = xx * s(y, 2, 0) + x * s(yx, 1, 0) + y * s(xx, 0, 1)
    u[2, -1] = xx * s(ymx, 1, 0) + x * s(ymx_then, 1, 0) + ym * s(xx, 0, -1)
    u[1, 2] = x * s(yy, 1, 0) + y * s(xy, 0, 1) + yy * s(x, 0, 2)
    u[1, -2] = x * s(ymym, 1, 0) + ym * s(xym, 0, -1) + ymym * s(x, 0, -2)
    return u


def kernel(
    sizes,
    p_hbm, coef_hbm, ccoef_hbm, r_hbm, d_hbm,
    q_ref, step_ref, growth_ref,
    pv, coef_ref, ccoef_ref, r_ref, d_ref,
    wct, wch, line, lanes_out, packs, packs_y, packs_d, strips,
    rx_next, rx_prev, rc_next, rc_prev, ry, rd,
    cb, hv, hyc, sums_ref, inner, weights, coarse_weights, dv, dk, ev, fv, mv, copies, totals,
    acc, acc_other, part, slots,
    load_sem, send_sem, recv_sem, group_send, group_recv,
):
    n_x, n_y = sizes
    levels, rows, cols = d_ref.shape
    half, tiles = pv.shape[0], cols // LANES
    crows, ccols = ccoef_ref.shape[1], ccoef_ref.shape[2]
    gx, gy, ma = lax.axis_index("gx"), lax.axis_index("gy"), lax.axis_index("ma")
    me = gx * n_y + gy
    group = n_x * n_y
    has = {
        (-1, 0): gx > 0, (1, 0): gx < n_x - 1, (0, -1): gy > 0, (0, 1): gy < n_y - 1,
    }
    for dx in (-1, 1):
        for dy in (-1, 1):
            has[(dx, dy)] = has[(dx, 0)] & has[(0, dy)]

    def turned(at, count):
        return [at] + [
            jnp.where(at + k >= count, at + k - count, at + k) for k in range(1, count)
        ]

    if group <= 16:
        peers = [(x, y) for x in turned(gx, n_x) for y in turned(gy, n_y)][1:]

    def each_peer(action):
        if group <= 16:
            for x, y in peers:
                action(x, y)
            return

        def body(step, carry):
            k = lax.rem(me + step, group)
            action(k // n_y, k % n_y)
            return carry

        lax.fori_loop(1, group, body, 0)

    def lanes_of(j):
        return slice(j * LANES, (j + 1) * LANES)

    own = pl.ds(EDGE, rows)
    fields = half * levels
    bands = wct.shape[1]
    spans = [(g, pl.ds(8 * g, min(8, half - 8 * g))) for g in range(cb.shape[3])]
    loads = []

    def load(src, dst):
        loads.append(pltpu.make_async_copy(src, dst, load_sem.at[len(loads)]))
        loads[-1].start()

    load(d_hbm, d_ref)
    for j in range(tiles):
        load(p_hbm.at[:, :, :, pl.ds(j * LANES, LANES)], pv.at[:, :, j, own])
    load(coef_hbm, coef_ref)
    load(ccoef_hbm, ccoef_ref)
    load(r_hbm, r_ref)
    early = len(loads)

    barrier = pltpu.get_barrier_semaphore()
    pl.semaphore_signal(barrier, inc=1, device_id={"ma": 1 - ma}, device_id_type=MESH)
    each_peer(
        lambda x, y: pl.semaphore_signal(
            barrier, inc=1, device_id={"gx": x, "gy": y}, device_id_type=MESH
        )
    )
    for side in (0, 1):
        for level in range(levels):
            for e in range(REACH):
                x = rows - 1 - e if side else e
                for g, span in spans:
                    load(p_hbm.at[span, level, x], cb.at[side, level, REACH + e, g, pl.ds(0, span.size)])

    def zero_if(absent, ref):
        @pl.when(absent)
        def _():
            ref[...] = jnp.zeros_like(ref)

    zero_if(gx == 0, rx_prev)
    zero_if(gx == 0, rc_prev)
    zero_if(gx == n_x - 1, rx_next)
    zero_if(gx == n_x - 1, rc_next)
    rest = -half % 8
    for g, span in spans:
        zero_if(gx == 0, cb.at[0, :, pl.ds(0, REACH), g, pl.ds(0, span.size)])
        zero_if(gx == n_x - 1, cb.at[1, :, pl.ds(0, REACH), g, pl.ds(0, span.size)])
    if rest:
        cb[:, :, :, cb.shape[3] - 1, 8 - rest :] = jnp.zeros((2, levels, 2 * REACH, rest, cols), F32)
    pv[:, :, :, :EDGE] = jnp.zeros((half, levels, tiles, EDGE, LANES), F32)
    pv[:, :, :, EDGE + rows :] = jnp.zeros((half, levels, tiles, EDGE, LANES), F32)
    zero_if(gx == 0, wct.at[pl.ds(HALO - REACH, REACH)])
    zero_if(gx == n_x - 1, wct.at[pl.ds(HALO + crows, REACH)])
    for x in (0, 2 * HALO + crows - 1):
        wct[x] = jnp.zeros((bands, 8, LANES), F32)
    for f in range(fields, 8 * bands):
        line[f * rows : (f + 1) * rows] = jnp.zeros((rows, ccols), F32)
    for side in (0, 1):
        dy = 2 * side - 1
        zero_if(jnp.logical_not(has[(0, dy)]), ry.at[side])
        zero_if(jnp.logical_not(has[(0, dy)]), packs_y.at[side])
        for way in (0, 1):
            zero_if(jnp.logical_not(has[(2 * way - 1, dy)]), rd.at[side, way])
            zero_if(jnp.logical_not(has[(2 * way - 1, dy)]), packs_d.at[side, way])

    moves = []

    def move(src, dst, dx, dy):
        slot = len(moves)
        target = {
            "gx": jnp.clip(gx + dx, 0, n_x - 1) if dx else gx,
            "gy": jnp.clip(gy + dy, 0, n_y - 1) if dy else gy,
        }
        copy = pltpu.make_async_remote_copy(
            src_ref=src, dst_ref=dst, send_sem=send_sem.at[slot], recv_sem=recv_sem.at[slot],
            device_id=target, device_id_type=MESH,
        )
        moves.append((copy, has[(dx, dy)], has[(-dx, -dy)]))

        @pl.when(has[(dx, dy)])
        def _():
            copy.start()

        return slot

    def arrive(slot):
        @pl.when(moves[slot][2])
        def _():
            moves[slot][0].wait_recv()

    def move_rows(level):
        slots_of = []
        for h in range(REACH):
            for g, span in spans:
                for side, x in ((1, h), (0, rows - 1 - h)):
                    dst = cb.at[side, level, h, g, pl.ds(0, span.size)]
                    slots_of.append(move(p_hbm.at[span, level, x], dst, 1 - 2 * side, 0))
        return slots_of

    for copy in loads[:early]:
        copy.wait()
    flane = lax.broadcasted_iota(jnp.int32, (rows, LANES), 1)
    blane = lax.broadcasted_iota(jnp.int32, (8, LANES), 1)
    lane = blane
    clane = lax.broadcasted_iota(jnp.int32, (crows, LANES), 1)
    fl = fr = jnp.zeros((rows, LANES), F32)
    cl = cr = jnp.zeros((crows, LANES), F32)
    for f in (0, 1):
        at = PASSES * f
        field = ccoef_ref[f]
        cl = jnp.where(
            clane >= at, pltpu.roll(field[:, :LANES], at, 1) if at else field[:, :LANES], cl
        )
        cr = jnp.where(clane >= at, pltpu.roll(field[:, ccols - LANES :], at + PASSES, 1), cr)
    for f in range(fields + 2 + levels):
        at = PASSES * f
        if f < fields:
            first = pv[f // levels, f % levels, 0, EDGE : EDGE + rows]
            last = pv[f // levels, f % levels, tiles - 1, EDGE : EDGE + rows]
        elif f < fields + 2:
            first = coef_ref[f - fields, :, :LANES]
            last = coef_ref[f - fields, :, cols - LANES :]
        else:
            first = d_ref[f - fields - 2, :, :LANES]
            last = d_ref[f - fields - 2, :, cols - LANES :]
        fl = jnp.where(flane >= at, pltpu.roll(first, at, 1) if at else first, fl)
        fr = jnp.where(flane >= at, pltpu.roll(last, at + PASSES, 1), fr)
    for side, (fine, small) in enumerate(((fl, cl), (fr, cr))):
        strips[side, 0:crows] = small
        strips[side, crows : crows + rows] = fine
        strips[side, crows + rows :] = small
    for level in range(levels):
        for j in range(tiles):
            here = d_ref[level, :, lanes_of(j)]
            there = d_ref[level, :, lanes_of((j + 1) % tiles)]
            dv[level, j, :EDGE] = jnp.zeros((EDGE, LANES), F32)
            dv[level, j, EDGE : EDGE + rows] = here
            dv[level, j, EDGE + rows :] = jnp.zeros((EDGE, LANES), F32)
            for k in (1, 2, 3):
                dk[level, k - 1, j] = jnp.where(
                    flane < LANES - k,
                    pltpu.roll(here, LANES - k, 1),
                    pltpu.roll(there, LANES - k, 1),
                )
            for t in range(len(ROWS)):
                ev[level, t, j, :EDGE] = jnp.zeros((EDGE, LANES), F32)
                ev[level, t, j, EDGE + rows :] = jnp.zeros((EDGE, LANES), F32)
    lin = lax.broadcasted_iota(jnp.int32, (LANES, LANES), 0)
    lout = lax.broadcasted_iota(jnp.int32, (LANES, LANES), 1)
    step = lax.rem(lout, PASSES)
    inside = lout < PASSES * fields
    for n, (side, ahead, k) in enumerate(MATRICES):
        if side:
            source = step + (LANES - PASSES if ahead else k - PASSES)
            hit = (lin == source) & (step >= PASSES - k) & inside
        else:
            source = step if ahead else step + (LANES - k)
            hit = (lin == source) & (step < k) & inside
        copies[n] = jnp.where(hit, 1.0, 0.0).astype(BF16)
    period = PASSES * levels
    hit = (lin - PASSES * (fields + 2) == lax.rem(lout, period)) & inside
    copies[COPIES] = jnp.where(hit, 1.0, 0.0).astype(BF16)
    for level in range(levels):
        source = lax.rem(lin, period) - PASSES * level
        for side in (0, 1):
            place = lout - (LANES - PASSES) * side
            hit = (source == place) & (place >= 0) & (place < PASSES) & (lin < PASSES * fields)
            totals[side, :, lanes_of(level)] = jnp.where(hit, 1.0, 0.0).astype(BF16)

    pl.semaphore_wait(barrier, group)
    e_moves = []
    for k, (src, count) in enumerate(((coef_hbm, 2), (d_hbm, levels))):
        span = pl.ds(2 * k, count)
        e_moves.append(move(src.at[:, pl.ds(0, HALO)], rx_next.at[span], -1, 0))
        e_moves.append(move(src.at[:, pl.ds(rows - HALO, HALO)], rx_prev.at[span], 1, 0))
    e_moves.append(move(ccoef_hbm.at[:, pl.ds(0, HALO)], rc_next, -1, 0))
    e_moves.append(move(ccoef_hbm.at[:, pl.ds(crows - HALO, HALO)], rc_prev, 1, 0))
    y_moves = []
    for side in (0, 1):
        dy = 2 * side - 1
        other = 1 - side
        y_moves.append(move(strips.at[side, pl.ds(0, crows + rows)], ry.at[other], 0, dy))
        y_moves.append(move(strips.at[side, pl.ds(0, crows + 8)], rd.at[other, 1], -1, dy))
        y_moves.append(
            move(strips.at[side, pl.ds(crows + rows - 8, crows + 8)], rd.at[other, 0], 1, dy)
        )

    pick = lax.broadcasted_iota(jnp.int32, (cols, ccols), 0) // RATIO
    gather = jnp.where(
        pick == lax.broadcasted_iota(jnp.int32, (cols, ccols), 1), 1.0 / RATIO**2, 0.0
    ).astype(BF16)
    batch = next(k for k in (5, 3, 2, 1) if half % k == 0)

    def restrict(n, carry):
        tall = batch * levels * rows
        values = jnp.concatenate(
            [
                (
                    pv[pl.ds(n * batch, batch), :, j, EDGE : EDGE + rows]
                    * d_ref[:, :, lanes_of(j)][None]
                ).reshape(tall, LANES)
                for j in range(tiles)
            ],
            axis=1,
        )
        line[pl.ds(pl.multiple_of(n * tall, 8), tall)] = split_dot(values, gather)
        return carry

    lax.fori_loop(0, half // batch, restrict, 0)
    for x in range(crows):
        for g in range(bands):
            value = None
            for k in range(RATIO):
                term = line[pl.ds(g * 8 * rows + RATIO * x + k, 8, stride=rows), :]
                value = term if k == 0 else value + term
            wct[HALO + x, g] = value

    for g in range(bands):
        for side in (0, 1):
            value = jnp.zeros((8, LANES), F32)
            for x in range(crows):
                at = PASSES * x
                turn = at + PASSES * side
                field = wct[HALO + x, g]
                value = jnp.where(blane >= at, pltpu.roll(field, turn, 1) if turn else field, value)
            packs[side, g] = value
    c_moves = []
    for side in (0, 1):
        dy = 2 * side - 1
        c_moves.append(move(packs.at[side], packs_y.at[1 - side], 0, dy))
        c_moves.append(move(packs.at[side], packs_d.at[1 - side, 1], -1, dy))
        c_moves.append(move(packs.at[side], packs_d.at[1 - side, 0], 1, dy))
    c_moves.append(
        move(wct.at[pl.ds(HALO, REACH)], wct.at[pl.ds(HALO + crows, REACH)], -1, 0)
    )
    c_moves.append(
        move(wct.at[pl.ds(HALO + crows - REACH, REACH)], wct.at[pl.ds(HALO - REACH, REACH)], 1, 0)
    )
    row_moves = [move_rows(level) for level in range(levels)]

    def products(n, carry):
        level = n // (rows // 8)
        at = pl.multiple_of(n % (rows // 8) * 8, 8)
        for j in range(0, tiles, 2):
            total = [[None] * len(PAIRS), [None] * len(PAIRS)]
            for m in range(half):
                here = [pv[m, level, (j + g) % tiles, pl.ds(at + EDGE, 8)] for g in range(3)]
                turned = [[pltpu.roll(v, LANES - k, 1) for v in here] for k in (1, 2, 3)]
                for g in range(2):
                    below = {
                        i: pv[m, level, j + g, pl.ds(at + EDGE + i, 8)] if i else here[g]
                        for i in range(-2, 4)
                    }
                    right = [here[g]] + [
                        jnp.where(lane < LANES - k, turned[k - 1][g], turned[k - 1][g + 1])
                        for k in (1, 2, 3)
                    ]
                    for t, (i, k) in enumerate(PAIRS):
                        v = below[i] * right[k]
                        total[g][t] = v if m == 0 else total[g][t] + v
            for g in range(2):
                for t in range(len(PAIRS)):
                    sums_ref[level, t, pl.ds(at, 8), lanes_of(j + g)] = total[g][t]
        return carry

    lax.fori_loop(0, levels * (rows // 8), products, 0)

    for slot in e_moves:
        arrive(slot)
    for slot in y_moves:
        arrive(slot)

    near = lax.broadcasted_iota(jnp.int32, (8, LANES), 0) < HALO
    for side in (0, 1):
        hyc[side, 0:crows] = ry[side, 0:crows]
        hyc[side, crows : crows + 8] = jnp.where(
            near, rd[side, 1, 0:8], rd[side, 0, crows : crows + 8]
        )
        hv[side, 0:EDGE] = rd[side, 0, 0:8]
        hv[side, EDGE : EDGE + rows] = ry[side, crows : crows + rows]
        hv[side, EDGE + rows :] = rd[side, 1, crows : crows + 8]

    def columns(ref, index, height):
        lane = lax.broadcasted_iota(jnp.int32, (height, LANES), 1)
        at = PASSES * index
        right = pltpu.roll(ref[1], LANES - at, 1)
        left = pltpu.roll(ref[0], LANES - PASSES - at, 1)
        return jnp.where(
            lane < PASSES, right, jnp.where(lane >= LANES - PASSES, left, 0.0)
        )

    def coarse_field(f):
        height = crows + 2 * HALO
        tall = jnp.concatenate(
            [ccoef_ref[f], jnp.concatenate([rc_next[f], rc_prev[f]], axis=0)], axis=0
        )
        return jnp.concatenate([tall, columns(hyc, f, height)], axis=1)

    ext_rows, ext_cols = rows + 2 * EDGE, cols + LANES

    def wide(main, index):
        pad = jnp.zeros((EDGE - HALO, cols), F32)
        tall = jnp.concatenate(
            [
                jnp.concatenate([pad, rx_prev[index]], axis=0),
                main,
                jnp.concatenate([rx_next[index], pad], axis=0),
            ],
            axis=0,
        )
        return jnp.concatenate([tall, columns(hv, fields + index, ext_rows)], axis=1)

    ends = [
        value.astype(jnp.int32)
        for value in (has[(-1, 0)], has[(1, 0)], has[(0, -1)], has[(0, 1)])
    ]
    row = lax.broadcasted_iota(jnp.int32, (ext_rows, ext_cols), 0) - EDGE
    col = lax.broadcasted_iota(jnp.int32, (ext_rows, ext_cols), 1)
    outside = (
        ((row < 0) & (ends[0] == 0))
        | ((row >= rows) & (ends[1] == 0))
        | ((col >= cols + LANES // 2) & (ends[2] == 0))
        | ((col >= cols) & (col < cols + LANES // 2) & (ends[3] == 0))
    )
    u = composite(wide(coef_ref[0], 0), wide(coef_ref[1], 1), jnp.where(outside, 0.0, 1.0))

    row = lax.broadcasted_iota(jnp.int32, (rows, cols), 0)
    col = lax.broadcasted_iota(jnp.int32, (rows, cols), 1)
    for t, (i, k) in enumerate(PAIRS):
        if i >= 0:
            value = shifted(u[i, -k], 0, k) if i and k else u[i, k]
            valid = (row < rows - i) & (col < cols - k)
        else:
            value = shifted(u[-i, k], i, 0)
            valid = (row >= -i) & (col < cols - k)
        inner[t] = jnp.where(valid, value[EDGE : EDGE + rows, :cols], 0.0)

    ecol = lax.broadcasted_iota(jnp.int32, (EDGE, cols), 1)
    d_wide = [wide(d_ref[level], 2 + level) for level in range(levels)]
    for side in (0, 1):
        span = slice(rows, rows + 2 * EDGE) if side else slice(0, 2 * EDGE)
        take = slice(0, EDGE) if side else slice(EDGE, 2 * EDGE)
        for n, (i, k) in enumerate(ACROSS):
            move_x = i if side else -i
            if side:
                value = u[i, k][span]
            else:
                value = shifted(u[i, -k][span], move_x, k)
            valid = (ecol + k >= 0) & (ecol + k < cols)
            value = jnp.where(valid, value[take, :cols], 0.0)
            for level in range(levels):
                near_d = shifted(d_wide[level][span], move_x, k)[take, :cols]
                weights[side, level, n] = value * near_d

    edge_sums = []
    for side in (0, 1):
        halo_d = split_dot(hv[side], copies[COPIES])
        weighted = hv[side] * halo_d
        for k in (1, 2, 3):
            away = PASSES - k
            turn = away if side else -away % LANES
            mv[side, k - 1] = pltpu.roll(weighted, turn, 1) if away else weighted
        value = jnp.zeros((rows, LANES), F32)
        for n in range(COPIES):
            which, ahead, k = MATRICES[n]
            if which != side:
                continue
            stack, steps = [], []
            for i in range(k - 3, 4 - k):
                if side and ahead and i >= 0:
                    w = u[i, k][:, cols - LANES : cols]
                elif side and not ahead and i < 0:
                    w = shifted(u[-i, -k][:, cols:], i, 0)
                elif not side and ahead and i > 0:
                    w = u[i, -k][:, :LANES]
                elif not side and not ahead and i <= 0:
                    w = shifted(u[-i, k][:, cols:], i, 0)
                else:
                    continue
                stack.append(w[EDGE : EDGE + rows])
                steps.append(i)
            w = split_dot(jnp.concatenate(stack, axis=0), copies[n])
            for t, i in enumerate(steps):
                value = value + w[t * rows : (t + 1) * rows] * mv[side, k - 1, EDGE + i : EDGE + i + rows]
        value = value * strips[side, crows : crows + rows]
        edge_sums.append(split_dot(value, totals[side]))

    def combine(n, carry):
        level = n // (rows // 8)
        at = pl.multiple_of(n % (rows // 8) * 8, 8)
        for j in range(tiles):
            d_right = [dv[level, j, pl.ds(at + EDGE, 8)]] + [
                dk[level, k - 1, j, pl.ds(at, 8)] for k in (1, 2, 3)
            ]
            d_below = {
                i: dv[level, j, pl.ds(at + EDGE + i, 8)] if i else d_right[0] for i in range(-2, 4)
            }
            up, across = {}, {}
            for t, (i, k) in enumerate(PAIRS):
                value = (
                    inner[t, pl.ds(at, 8), lanes_of(j)]
                    * sums_ref[level, t, pl.ds(at, 8), lanes_of(j)]
                )
                term = value * d_right[k]
                up[i] = up[i] + term if i in up else term
                if i or k:
                    term = value * d_below[i]
                    across[k] = across[k] + term if k in across else term
            acc[level, pl.ds(at, 8), lanes_of(j)] = up[0] + across[0]
            for t, i in enumerate(ROWS):
                ev[level, t, j, pl.ds(at + EDGE, 8)] = up[i]
            for k in (1, 2, 3):
                fv[level, k - 1, j, pl.ds(at, 8)] = across[k]
        return carry

    lax.fori_loop(0, levels * (rows // 8), combine, 0, unroll=2)

    def collect(n, carry):
        level = n // (rows // 8)
        at = pl.multiple_of(n % (rows // 8) * 8, 8)
        turned = [
            [pltpu.roll(fv[level, k - 1, j, pl.ds(at, 8)], k, 1) for j in range(tiles)]
            for k in (1, 2, 3)
        ]
        for j in range(tiles):
            total = acc[level, pl.ds(at, 8), lanes_of(j)]
            for t, i in enumerate(ROWS):
                total = total + ev[level, t, j, pl.ds(at + EDGE - i, 8)]
            for k in (1, 2, 3):
                total = total + jnp.where(lane >= k, turned[k - 1][j], turned[k - 1][j - 1])
            acc[level, pl.ds(at, 8), lanes_of(j)] = total
        return carry

    lax.fori_loop(0, levels * (rows // 8), collect, 0, unroll=2)
    for level in range(levels):
        at = slice(level * LANES, (level + 1) * LANES)
        acc[level, :, :LANES] += edge_sums[0][:, at]
        acc[level, :, cols - LANES :] += edge_sums[1][:, at]

    for slot in c_moves:
        arrive(slot)
    for k, value in enumerate(
        stencil_weights(coarse_field(0), coarse_field(1), crows, ccols, *ends)
    ):
        coarse_weights[k] = value
    for x in range(-REACH, crows + REACH):
        for g in range(bands):
            way = 0 if x < 0 else 1
            inner_row = 0 <= x < crows
            left = packs_y[0, g] if inner_row else packs_d[0, way, g]
            right = packs_y[1, g] if inner_row else packs_d[1, way, g]
            at = PASSES * (x % crows)
            if at:
                right = pltpu.roll(right, LANES - at, 1)
            left = pltpu.roll(left, LANES - PASSES - at, 1)
            wch[0, HALO + x, g] = jnp.where(
                blane < PASSES, right, jnp.where(blane >= LANES - PASSES, left, 0.0)
            )
    for step in range(PASSES):
        low = HALO - REACH + 1 + step
        source = [wct, wch.at[0]] if step == 0 else [wch.at[2 * step - 1], wch.at[2 * step]]
        last = step == PASSES - 1

        def coarse_row(x, carry):
            w = [
                [coarse_weights[k, pl.ds((x + crows + HALO) % (crows + 2 * HALO), 1),
                                lanes_of(q)] for k in range(5)]
                for q in range(1 if last else 2)
            ]
            for g in range(bands):
                here = [source[q][x, g] for q in (0, 1)]
                ahead = [pltpu.roll(v, LANES - 1, 1) for v in here]
                back = [pltpu.roll(v, 1, 1) for v in here]
                for q in range(1 if last else 2):
                    value = (
                        w[q][0] * here[q]
                        + w[q][1] * source[q][x + 1, g]
                        + w[q][2] * source[q][x - 1, g]
                        + w[q][3] * jnp.where(blane < LANES - 1, ahead[q], ahead[1 - q])
                        + w[q][4] * jnp.where(blane >= 1, back[q], back[1 - q])
                    )
                    if last:
                        at = pl.multiple_of(((x - HALO) * bands + g) * 8, 8)
                        line[pl.ds(at, 8)] = value
                    else:
                        wch[2 * step + 1 + q, x, g] = value
            return carry

        for x in range(low, crows + 2 * HALO - low):
            coarse_row(x, 0)
    spread = jnp.where(
        lax.broadcasted_iota(jnp.int32, (ccols, cols), 1) // RATIO
        == lax.broadcasted_iota(jnp.int32, (ccols, cols), 0),
        1.0, 0.0,
    ).astype(BF16)
    wide_rows = split_dot(line[pl.ds(0, crows * bands * 8)], spread)
    for j in range(tiles):
        lanes_out[j] = wide_rows[:, lanes_of(j)]

    upper = lax.broadcasted_iota(jnp.int32, (8, LANES), 0) < RATIO

    def add_coarse(n, carry):
        level, t = n // (rows // 8), n % (rows // 8)
        at = pl.multiple_of(t * 8, 8)
        for j in range(tiles):
            total = None
            for m in range(half):
                base = 2 * t * (8 * bands) + m * levels + level
                a = jnp.broadcast_to(lanes_out[j, pl.ds(base, 1)], (8, LANES))
                b = jnp.broadcast_to(lanes_out[j, pl.ds(base + 8 * bands, 1)], (8, LANES))
                v = pv[m, level, j, pl.ds(at + EDGE, 8)] * jnp.where(upper, a, b)
                total = v if m == 0 else total + v
            acc[level, pl.ds(at, 8), lanes_of(j)] += total
        return carry

    lax.fori_loop(0, levels * (rows // 8), add_coarse, 0, unroll=2)

    for copy in loads[early:]:
        copy.wait()
    swaps = []
    for level in range(levels):
        for slot in row_moves[level]:
            arrive(slot)
        for side in (0, 1):
            for j in range(tiles):
                total = [None] * REACH
                for g in range(cb.shape[3]):
                    def tile(r, at):
                        return cb[side, level, r, g, :, lanes_of(at % tiles)]

                    halo = {}
                    for h in range(REACH):
                        halo[h, 0] = tile(h, j)
                        for k in range(1, REACH - h):
                            halo[h, k] = jnp.where(
                                lane < LANES - k,
                                pltpu.roll(tile(h, j), LANES - k, 1),
                                pltpu.roll(tile(h, j + 1), LANES - k, 1),
                            )
                            halo[h, -k] = jnp.where(
                                lane >= k,
                                pltpu.roll(tile(h, j), k, 1),
                                pltpu.roll(tile(h, j - 1), k, 1),
                            )
                    for e in range(REACH):
                        x = EDGE - 1 - e if side else e
                        value = None
                        for h in range(REACH - e):
                            i = e + h + 1
                            for k in range(i - 3, 4 - i):
                                w = weights[side, level, ACROSS.index((i, k)), x : x + 1, lanes_of(j)]
                                term = w * halo[h, k]
                                value = term if value is None else value + term
                        value = value * tile(REACH + e, j)
                        total[e] = value if g == 0 else total[e] + value
                for e in range(REACH):
                    x = rows - 1 - e if side else e
                    acc[level, x : x + 1, lanes_of(j)] += jnp.sum(total[e], axis=0, keepdims=True)
        slot = len(moves) + level
        swaps.append(
            pltpu.make_async_remote_copy(
                src_ref=acc.at[level], dst_ref=acc_other.at[level], send_sem=send_sem.at[slot],
                recv_sem=recv_sem.at[slot], device_id={"ma": 1 - ma}, device_id_type=MESH,
            )
        )
        swaps[level].start()

    for copy in swaps:
        copy.wait_recv()
    d, r = d_ref[...], r_ref[...]
    q = d + (acc[...] + acc_other[...]) * (1.0 / (MEMBERS - 1))
    q_ref[...] = q

    def total_row(value):
        flat = value.reshape(levels * rows // 8, 8, cols)
        tile = jnp.sum(flat, axis=0)
        narrow = tile[:, :LANES]
        for k in range(1, cols // LANES):
            narrow = narrow + tile[:, k * LANES : (k + 1) * LANES]
        return jnp.sum(narrow, axis=0, keepdims=True)

    row = lax.broadcasted_iota(jnp.int32, (8, LANES), 0)
    packed = jnp.zeros((8, LANES), F32)
    for k, value in enumerate((r * r, d * q, r * q, q * q)):
        packed = jnp.where(row == k, total_row(value), packed)
    part[...] = packed
    slots[me] = packed

    def to_peer(x, y):
        k = x * n_y + y
        return pltpu.make_async_remote_copy(
            src_ref=part, dst_ref=slots.at[me], send_sem=group_send.at[k],
            recv_sem=group_recv.at[me],
            device_id={"gx": x, "gy": y}, device_id_type=MESH,
        )

    def from_peer(x, y):
        k = x * n_y + y
        return pltpu.make_async_remote_copy(
            src_ref=part, dst_ref=slots.at[k], send_sem=group_send.at[k],
            recv_sem=group_recv.at[k],
            device_id={"gx": x, "gy": y}, device_id_type=MESH,
        )

    each_peer(lambda x, y: to_peer(x, y).start())
    for copy in swaps:
        copy.wait_send()
    for copy, sends, _ in moves:
        @pl.when(sends)
        def _():
            copy.wait_send()
    each_peer(lambda x, y: from_peer(x, y).wait_recv())
    sums = jnp.sum(jnp.sum(slots[...], axis=0), axis=1, keepdims=True)
    norm_old, curvature, cross, image = (sums[k : k + 1] for k in range(4))
    step_length = norm_old / curvature
    norm_new = norm_old + step_length * (step_length * image - 2.0 * cross)
    step_ref[...] = jnp.broadcast_to(step_length, (1, cols))
    growth_ref[...] = jnp.broadcast_to(norm_new / norm_old, (1, cols))
    each_peer(lambda x, y: to_peer(x, y).wait_send())


def local(n_x, n_y, perturbations, coefficients, coarse_coefficients, iterate, residual, direction):
    half, levels, rows, cols = perturbations.shape
    _, crows, ccols = coarse_coefficients.shape
    group = n_x * n_y
    groups = -(-half // 8)
    bands = -(-half * levels // 8)
    n_moves = 6 + 2 * REACH * levels * groups + 6 + 8 + levels
    vmem = pl.BlockSpec(memory_space=pltpu.VMEM)
    q, step_length, growth = pl.pallas_call(
        functools.partial(kernel, (n_x, n_y)),
        out_shape=(
            jax.ShapeDtypeStruct((levels, rows, cols), F32),
            jax.ShapeDtypeStruct((1, cols), F32),
            jax.ShapeDtypeStruct((1, cols), F32),
        ),
        in_specs=[pl.BlockSpec(memory_space=pltpu.HBM)] * 5,
        out_specs=(vmem, vmem, vmem),
        scratch_shapes=[
            pltpu.VMEM((half, levels, cols // LANES, rows + 2 * EDGE, LANES), F32),
            pltpu.VMEM((2, rows, cols), F32),
            pltpu.VMEM((2, crows, ccols), F32),
            pltpu.VMEM((levels, rows, cols), F32),
            pltpu.VMEM((levels, rows, cols), F32),
            pltpu.VMEM((crows + 2 * HALO, bands, 8, LANES), F32),
            pltpu.VMEM((2 * PASSES - 1, crows + 2 * HALO, bands, 8, LANES), F32),
            pltpu.VMEM((8 * bands * rows, ccols), F32),
            pltpu.VMEM((cols // LANES, 8 * bands * crows, LANES), F32),
            pltpu.VMEM((2, bands, 8, LANES), F32),
            pltpu.VMEM((2, bands, 8, LANES), F32),
            pltpu.VMEM((2, 2, bands, 8, LANES), F32),
            pltpu.VMEM((2, rows + 2 * crows, LANES), F32),
            pltpu.VMEM((2 + levels, HALO, cols), F32),
            pltpu.VMEM((2 + levels, HALO, cols), F32),
            pltpu.VMEM((2, HALO, ccols), F32),
            pltpu.VMEM((2, HALO, ccols), F32),
            pltpu.VMEM((2, rows + crows, LANES), F32),
            pltpu.VMEM((2, 2, crows + 8, LANES), F32),
            pltpu.VMEM((2, levels, 2 * REACH, groups, 8, cols), F32),
            pltpu.VMEM((2, rows + 2 * EDGE, LANES), F32),
            pltpu.VMEM((2, crows + 2 * HALO, LANES), F32),
            pltpu.VMEM((levels, len(PAIRS), rows, cols), F32),
            pltpu.VMEM((len(PAIRS), rows, cols), F32),
            pltpu.VMEM((2, levels, len(ACROSS), EDGE, cols), F32),
            pltpu.VMEM((5, crows + 2 * HALO, ccols + LANES), F32),
            pltpu.VMEM((levels, cols // LANES, rows + 2 * EDGE, LANES), F32),
            pltpu.VMEM((levels, 3, cols // LANES, rows, LANES), F32),
            pltpu.VMEM((levels, len(ROWS), cols // LANES, rows + 2 * EDGE, LANES), F32),
            pltpu.VMEM((levels, 3, cols // LANES, rows, LANES), F32),
            pltpu.VMEM((2, 3, rows + 2 * EDGE, LANES), F32),
            pltpu.VMEM((COPIES + 1, LANES, LANES), BF16),
            pltpu.VMEM((2, LANES, levels * LANES), BF16),
            pltpu.VMEM((levels, rows, cols), F32),
            pltpu.VMEM((levels, rows, cols), F32),
            pltpu.VMEM((8, LANES), F32),
            pltpu.VMEM((group, 8, LANES), F32),
            pltpu.SemaphoreType.DMA((4 + cols // LANES + 2 * levels * REACH * groups,)),
            pltpu.SemaphoreType.DMA((n_moves,)),
            pltpu.SemaphoreType.DMA((n_moves,)),
            pltpu.SemaphoreType.DMA((group,)),
            pltpu.SemaphoreType.DMA((group,)),
        ],
        compiler_params=pltpu.CompilerParams(
            collective_id=0, has_side_effects=True, vmem_limit_bytes=62 << 20
        ),
    )(perturbations, coefficients, coarse_coefficients, residual, direction)
    new_iterate = iterate + step_length * direction
    new_residual = residual - step_length * q
    new_direction = new_residual + growth * direction
    return (new_iterate, new_residual, new_direction)


def solution(mesh):
    cell = P(None, "gx", "gy")
    return jax.shard_map(
        functools.partial(local, mesh.shape["gx"], mesh.shape["gy"]),
        mesh=mesh,
        in_specs=(P("ma", None, "gx", "gy"), cell, cell, cell, cell, cell),
        out_specs=(cell, cell, cell),
        check_vma=False,
    )
```
